32 devices in a mesh: leaf: 16 (over z, y, x), rhs: 2 (over core).
Axes of the slice: x: 2, y: 2, z: 4, core: 2. Of those that a mesh axis runs over, the one named last changes fastest.
Arguments:
- rhs_block: float32 [16384, 2048], P(('leaf', 'rhs')), may hold values from -6 to 6
- leaf_inverse: float32 [16384, 1024], P('leaf', 'rhs'), may hold values from -0.1875 to 0.1875
- leaf_basis: float32 [16384, 128], P('leaf'), may hold values from -0.1875 to 0.1875
- couple_one: float32 [2048, 512], P('leaf'), may hold values from -0.25 to 0.25
- basis_one: float32 [2048, 128], P('leaf'), may hold values from -0.25 to 0.25
- couple_two: float32 [512, 512], P('leaf'), may hold values from -0.25 to 0.25
- basis_two: float32 [512, 128], P('leaf'), may hold values from -0.25 to 0.25
- root_inverse: float32 [128, 128], P('leaf'), may hold values from -0.5 to 0.5
- leaf_slot: int32 [16], replicated, may hold values from 0 to 3, as said below
- node_slot: int32 [4], replicated, may hold values from 0 to 3, as said below
Outputs:
- solution: float32 [16384, 2048], P('leaf', 'rhs')
The draws below stay inside these ranges and needn't reach their ends.
Inputs may be any that keep to these rules, and one draw needn't show every extreme that they name: `leaf_slot`: in every aligned group of four leaves the four entries are a permutation of 0 to 3. `node_slot`: in every aligned group of four first-level nodes the four entries are a permutation of 0 to 3.
All inputs are finite; a program needn't handle non-finite values.
Results may differ from the reference program's by a relative error of at most 0.00007.
Values sent between devices are 32-bit elements; how exact they have to be, the bound alone decides.
No kernel may reach another device: no remote copies, remote signals or barrier semaphores. Data moves between devices by JAX's collectives and lax.ppermute only.
A program may use at most 128 MiB of HBM per device.

```python
import jax
import jax.numpy as jnp
from jax import lax

LEAF = 1024
RANK = 128
COUPLE = 512
RHS = 2048
NPTS = 16384
TOP = 128
N_LEAF = 16


def group_perms(key, groups):
    subkeys = jax.random.split(key, groups)
    return jax.vmap(lambda subkey: jax.random.permutation(subkey, 4))(subkeys).reshape(-1).astype(jnp.int32)


def draw_leaf_slot(key, part):
    return group_perms(jax.random.fold_in(key, 11), N_LEAF // 4)


def draw_node_slot(key, part):
    return group_perms(jax.random.fold_in(key, 23), N_LEAF // 16)


def shard_levels(stream_key, extent, pieces, least, high):
    factor_of, own = 1.0, jax.random.fold_in(stream_key, 6)
    for dim, shards_of in pieces:
        steps = jnp.exp(jax.random.uniform(jax.random.fold_in(own, dim), (shards_of,), jnp.float32, least / len(pieces), high / len(pieces)))
        factor_of = factor_of * jnp.repeat(steps, extent[dim] // shards_of).reshape([-1 if axis == dim else 1 for axis in range(len(extent))])
    return factor_of


def centred(own_key, dims, width, most, cuts=(), kind=jnp.bfloat16):
    drawn = jax.random.normal(own_key, dims, jnp.float32) * width
    if len(cuts) > 0:
        drawn = shard_levels(own_key, dims, cuts, -0.22, 0.18) * drawn
    return jnp.clip(drawn, min=-most, max=most).astype(kind)


def setup_inputs(seed: int = 0) -> dict:
    key_of = jax.random.split(jax.random.key(seed), 11)
    rhs_block = centred(key_of[0], (NPTS, RHS), 1.0, 6.0, ((0, 32),), jnp.float32)
    leaf_inverse = centred(key_of[1], (NPTS, LEAF), LEAF ** -0.5, 0.1875, ((0, 16), (1, 2)), jnp.float32)
    leaf_basis = centred(key_of[2], (NPTS, RANK), LEAF ** -0.5, 0.1875, ((0, 16),), jnp.float32)
    couple_one = centred(key_of[3], (N_LEAF * RANK, COUPLE), COUPLE ** -0.5, 0.25, ((0, 16),), jnp.float32)
    basis_one = centred(key_of[4], (N_LEAF * RANK, RANK), COUPLE ** -0.5, 0.25, ((0, 16),), jnp.float32)
    couple_two = centred(key_of[5], (N_LEAF * RANK // 4, COUPLE), COUPLE ** -0.5, 0.25, ((0, 16),), jnp.float32)
    basis_two = centred(key_of[6], (N_LEAF * RANK // 4, RANK), COUPLE ** -0.5, 0.25, ((0, 16),), jnp.float32)
    root_inverse = centred(key_of[7], (TOP, TOP), TOP ** -0.5, 0.5, ((0, 16),), jnp.float32)
    leaf_slot = draw_leaf_slot(jax.random.fold_in(key_of[10], 71), 0)
    node_slot = draw_node_slot(jax.random.fold_in(key_of[10], 71), 0)
    return dict(rhs_block=rhs_block, leaf_inverse=leaf_inverse, leaf_basis=leaf_basis, couple_one=couple_one, basis_one=basis_one, couple_two=couple_two, basis_two=basis_two, root_inverse=root_inverse, leaf_slot=leaf_slot, node_slot=node_slot)


def place_groups(coeffs, slots):
    count = coeffs.shape[0] // 4
    onehot = (slots.reshape(count, 4)[:, :, None] == jnp.arange(4, dtype=jnp.int32)[None, None, :]).astype(jnp.float32)
    grouped = coeffs.reshape(count, 4, RANK, coeffs.shape[-1])
    placed = jnp.einsum('gjs,gjrk->gsrk', onehot, grouped, precision=lax.Precision.HIGHEST)
    return placed.reshape(count, 4 * RANK, coeffs.shape[-1])


def pick_groups(vectors, slots):
    count = vectors.shape[0]
    onehot = (slots.reshape(count, 4)[:, :, None] == jnp.arange(4, dtype=jnp.int32)[None, None, :]).astype(jnp.float32)
    spans = vectors.reshape(count, 4, RANK, vectors.shape[-1])
    picked = jnp.einsum('gjs,gsrk->gjrk', onehot, spans, precision=lax.Precision.HIGHEST)
    return picked.reshape(count * 4, RANK, vectors.shape[-1])


def reference(rhs_block, leaf_inverse, leaf_basis, couple_one, basis_one, couple_two, basis_two, root_inverse, leaf_slot, node_slot):
    precise = lax.Precision.HIGHEST
    columns = rhs_block.shape[1]
    blocks = rhs_block.reshape(N_LEAF, LEAF, columns)
    inverses = leaf_inverse.reshape(N_LEAF, LEAF, LEAF)
    leaf_solve = lax.map(lambda operands: jnp.dot(operands[0], operands[1], precision=precise), (inverses, blocks))
    bases = leaf_basis.reshape(N_LEAF, LEAF, RANK)
    leaf_coeff = jnp.einsum('nlr,nlk->nrk', bases, leaf_solve, precision=precise)
    stack_one = place_groups(leaf_coeff, leaf_slot)
    couple_first = couple_one.reshape(N_LEAF // 4, 4 * RANK, 4 * RANK)
    basis_first = basis_one.reshape(N_LEAF // 4, 4 * RANK, RANK)
    node_solve = jnp.einsum('pab,pbk->pak', couple_first, stack_one, precision=precise)
    node_coeff = jnp.einsum('par,pak->prk', basis_first, node_solve, precision=precise)
    stack_two = place_groups(node_coeff, node_slot)
    couple_second = couple_two.reshape(N_LEAF // 16, 4 * RANK, 4 * RANK)
    basis_second = basis_two.reshape(N_LEAF // 16, 4 * RANK, RANK)
    upper_solve = jnp.einsum('pab,pbk->pak', couple_second, stack_two, precision=precise)
    upper_coeff = jnp.einsum('par,pak->prk', basis_second, upper_solve, precision=precise)
    root_solve = jnp.dot(root_inverse, upper_coeff.reshape(-1, columns), precision=precise)
    upper_down = upper_solve - jnp.einsum('par,prk->pak', basis_second, root_solve.reshape(N_LEAF // 16, RANK, columns), precision=precise)
    node_down = node_solve - jnp.einsum('par,prk->pak', basis_first, pick_groups(upper_down, node_slot), precision=precise)
    solution = leaf_solve - jnp.einsum('nlr,nrk->nlk', bases, pick_groups(node_down, leaf_slot), precision=precise)
    return solution.reshape(N_LEAF * LEAF, columns)
```

```python
import jax
import jax.numpy as jnp
from jax import lax
from jax.sharding import PartitionSpec as P

PRECISE = lax.Precision.HIGH


def mul(left, right):
    return jnp.dot(left, right, precision=PRECISE, preferred_element_type=jnp.float32)


def mul_t(left, right):
    return lax.dot_general(
        left, right, (((0,), (0,)), ((), ())), precision=PRECISE, preferred_element_type=jnp.float32
    )


def swap(block, bits):
    count = lax.axis_size("leaf")
    return lax.ppermute(block, "leaf", [(low, low ^ bits) for low in range(count)])


def swap_core(block):
    return lax.ppermute(block, "rhs", [(0, 1), (1, 0)])


def rows_of(array, start, count):
    return lax.dynamic_slice_in_dim(array, start, count, 0)


def columns_of(array, start, count):
    return lax.dynamic_slice_in_dim(array, start, count, 1)


def both_halves(mine, other, core):
    lower = jnp.where(core == 0, mine, other)
    upper = jnp.where(core == 0, other, mine)
    return jnp.concatenate([lower, upper], 1)


def in_slots(blocks, slots, own):
    arity = len(blocks)
    stacked = jnp.stack(blocks)
    members = jnp.arange(arity, dtype=jnp.int32)
    placed = []
    for place in range(arity):
        member = jnp.sum(jnp.where(slots == place, members, 0))
        placed.append(lax.dynamic_index_in_dim(stacked, member ^ own, 0, keepdims=False))
    return jnp.concatenate(placed, 0)


def per_device(
    rhs_block,
    leaf_inverse,
    leaf_basis,
    couple_one,
    basis_one,
    couple_two,
    basis_two,
    root_inverse,
    leaf_slot,
    node_slot,
):
    position = lax.axis_index("leaf")
    devices = lax.axis_size("leaf")
    core = lax.axis_index("rhs")
    rank = leaf_basis.shape[1]
    couple = couple_one.shape[1]
    arity = couple // rank
    group = arity * arity
    tops = devices // group
    half = rhs_block.shape[1] // lax.axis_size("rhs")
    width = half // arity
    member = position % arity
    node = position // arity
    node_member = node % arity

    projected = mul_t(leaf_basis, leaf_inverse)
    own_rhs = columns_of(rhs_block, core * half, half)
    other_rhs = columns_of(rhs_block, (1 - core) * half, half)
    coeff_send = mul(projected, other_rhs)
    coeff_own = mul(projected, own_rhs)
    coeff = coeff_own + swap_core(coeff_send)

    joined = jnp.concatenate([couple_one, basis_one], 1)
    joined_half = rows_of(joined, core * (rank // 2), rank // 2)
    got = jnp.stack([swap(joined_half, bits) for bits in range(1, arity)])
    got_other = swap_core(got)
    joined_all = jnp.concatenate([joined[None], both_halves(got, got_other, core)], 0)
    couple_all = joined_all[:, :, :couple].reshape(arity * rank, couple)
    basis_all = joined_all[:, :, couple:].reshape(arity * rank, rank)
    reduced_one = mul_t(basis_all, couple_all)

    share = couple_two.shape[0]
    root_share = root_inverse.shape[0]
    joined_two = jnp.concatenate([couple_two, basis_two], 1)
    two_by_z = jnp.stack([joined_two] + [swap(joined_two, arity * bits) for bits in range(1, arity)])
    root_by_z = jnp.stack([root_inverse] + [swap(root_inverse, arity * bits) for bits in range(1, arity)])

    pieces = [columns_of(coeff, (member ^ bits) * width, width) for bits in range(arity)]
    pieces = [pieces[0]] + [swap(pieces[bits], bits) for bits in range(1, arity)]
    stack_one = in_slots(pieces, rows_of(leaf_slot, node * arity, arity), member)
    node_coeff = mul(reduced_one, stack_one)

    uppers = [node_coeff] + [swap(node_coeff, arity * bits) for bits in range(1, arity)]
    stack_two = in_slots(
        uppers, rows_of(node_slot, node // arity * arity, arity), node_member
    )

    two_half = lax.dynamic_slice_in_dim(two_by_z, core * (share // 2), share // 2, 1)
    two_half = two_half.reshape(arity * (share // 2), -1)
    two_got = jnp.stack([swap(two_half, bits) for bits in range(1, arity)])
    two_other = swap_core(two_got)
    two_got = two_got.reshape(3, arity, share // 2, -1)
    two_other = two_other.reshape(3, arity, share // 2, -1)
    lower = jnp.where(core == 0, two_got, two_other)
    upper = jnp.where(core == 0, two_other, two_got)
    two_all = jnp.concatenate([two_by_z[None], jnp.concatenate([lower, upper], 2)], 0)
    root_all = jnp.stack(
        [root_by_z] + [swap(root_by_z, bits) for bits in range(1, arity)]
    )
    order = jnp.arange(arity, dtype=jnp.int32)
    two_all = jnp.take(jnp.take(two_all, order ^ member, axis=0), order ^ node_member, axis=1)
    root_all = jnp.take(jnp.take(root_all, order ^ member, axis=0), order ^ node_member, axis=1)
    two_all = two_all.transpose(1, 0, 2, 3).reshape(arity * arity * share, -1)
    root_all = root_all.transpose(1, 0, 2, 3).reshape(rank, -1)
    reduced_two = mul_t(two_all[:, couple:], two_all[:, :couple])
    own_node = rows_of(node_slot, node, 1)[0]
    two_rows = rows_of(two_all, own_node * rank, rank)

    if tops == 1:
        root_coeff = mul(root_all, reduced_two)
        down_map = two_rows[:, :couple] - mul(two_rows[:, couple:], root_coeff)
        upper_down = mul(down_map, stack_two)
    else:
        upper_coeff = mul(reduced_two, stack_two)
        top_member = position // group
        tops_coeff = jnp.stack(
            [upper_coeff] + [swap(upper_coeff, group * bits) for bits in range(1, tops)]
        )
        tops_coeff = jnp.take(tops_coeff, jnp.arange(tops, dtype=jnp.int32) ^ top_member, axis=0)
        root_solve = mul(root_all, tops_coeff.reshape(tops * rank, -1))
        upper_down = mul(two_rows[:, :couple], stack_two) - mul(two_rows[:, couple:], root_solve)

    node_down = mul(couple_all, stack_one) - mul(basis_all, upper_down)
    node_down = node_down.reshape(arity, rank, width)
    slots = rows_of(leaf_slot, node * arity, arity)
    back = []
    for bits in range(arity):
        place = lax.dynamic_index_in_dim(slots, member ^ bits, 0, keepdims=False)
        block = lax.dynamic_index_in_dim(node_down, place ^ member, 0, keepdims=False)
        back.append(block if bits == 0 else swap(block, bits))
    back = jnp.take(jnp.stack(back), order ^ member, axis=0)
    leaf_down = back.transpose(1, 0, 2).reshape(rank, half)

    solve_send = mul(leaf_inverse, other_rhs)
    solve_own = mul(leaf_inverse, own_rhs)
    leaf_solve = solve_own + swap_core(solve_send)
    return leaf_solve - mul(leaf_basis, leaf_down)


def solution(mesh):
    return jax.shard_map(
        per_device,
        mesh=mesh,
        in_specs=(
            P(("leaf", "rhs"), None),
            P("leaf", "rhs"),
            P("leaf", None),
            P("leaf", None),
            P("leaf", None),
            P("leaf", None),
            P("leaf", None),
            P("leaf", None),
            P(),
            P(),
        ),
        out_specs=P("leaf", "rhs"),
        check_vma=False,
    )
```

```python
import functools

import jax
import jax.numpy as jnp
from jax import lax
from jax.experimental import pallas as pl
from jax.experimental.pallas import tpu as pltpu
from jax.sharding import PartitionSpec as P

F32 = jnp.float32
BF16 = jnp.bfloat16


def split(value):
    high = value.astype(BF16)
    return high, (value - high.astype(F32)).astype(BF16)


def dot(left, right):
    return jnp.dot(left, right, preferred_element_type=F32)


def dot_parts(left_high, left_low, right_high, right_low):
    rows = left_high.shape[0]
    both = dot(jnp.concatenate([left_high, left_low], 0), right_high)
    return both[:rows] + both[rows:] + dot(left_high, right_low)


def dot_split(left, right):
    return dot_parts(*split(left), *split(right))


def whole(shape):
    return pl.BlockSpec(shape, lambda *_: (0,) * len(shape))


def call(body, out_shapes, scalars, operands, flops, limit_mib=16, scratch=()):
    moved = sum(o.size * o.dtype.itemsize for o in list(operands) + list(out_shapes))
    return pl.pallas_call(
        body,
        out_shape=out_shapes,
        grid_spec=pltpu.PrefetchScalarGridSpec(
            num_scalar_prefetch=len(scalars),
            grid=(1,),
            in_specs=[whole(o.shape) for o in operands],
            out_specs=[whole(o.shape) for o in out_shapes],
            scratch_shapes=scratch,
        ),
        compiler_params=pltpu.CompilerParams(vmem_limit_bytes=limit_mib << 20),
        cost_estimate=pl.CostEstimate(flops=flops, bytes_accessed=moved, transcendentals=0),
    )(*scalars, *operands)


def struct(*shape):
    return jax.ShapeDtypeStruct(shape, F32)


def coeff_send_body(
    ids, basis, inverse, rhs, couple_one, basis_one, couple_two, basis_two, root,
    send, projected, joined, packed, parts,
):
    rank = basis.shape[1]
    couple = couple_one.shape[1]

    @pl.when(pl.program_id(0) == 0)
    def _():
        value = dot_split(basis[...].T, inverse[...])
        projected[...] = value
        high, low = split(value)
        parts[:rank] = high
        parts[rank:] = low
        joined[:, :couple] = couple_one[...]
        joined[:, couple:] = basis_one[...]
        share = couple_two.shape[0]
        packed[...] = jnp.zeros_like(packed)
        packed[:share, :couple] = couple_two[...]
        packed[:share, couple:] = basis_two[...]
        rows, wide = root.shape
        piece = min(wide, couple)
        for part in range(wide // piece):
            packed[share + part * rows : share + (part + 1) * rows, :piece] = root[
                :, part * piece : (part + 1) * piece
            ]

    high, low = split(rhs[...])
    both = dot(parts[...], high)
    send[...] = both[:rank] + both[rank:] + dot(parts[:rank], low)


def coeff_own_body(ids, projected, rhs, own, parts):
    rank = projected.shape[0]

    @pl.when(pl.program_id(0) == 0)
    def _():
        high, low = split(projected[...])
        parts[:rank] = high
        parts[rank:] = low

    high, low = split(rhs[...])
    both = dot(parts[...], high)
    own[...] = both[:rank] + both[rank:] + dot(parts[:rank], low)


def leaf_body(add, ids, inverse, rhs, *rest):
    if add:
        extra, out, right_high, right_low = rest
    else:
        out, right_high, right_low = rest

    @pl.when(pl.program_id(0) == 0)
    def _():
        high, low = split(rhs[...])
        right_high[...] = high
        right_low[...] = low

    left_high, left_low = split(inverse[...])
    value = (
        dot(left_high, right_high[...]) + dot(left_high, right_low[...]) + dot(left_low, right_high[...])
    )
    out[...] = value + extra[...] if add else value


def leaf_product(ids, inverse, rhs, half, own, extra=None):
    rows, depth = inverse.shape
    steps = 4
    tile = rows // steps
    side = (lambda i, ids: (0, ids[1])) if own else (lambda i, ids: (0, 1 - ids[1]))
    in_specs = [pl.BlockSpec((tile, depth), lambda i, ids: (i, 0)), pl.BlockSpec((depth, half), side)]
    operands = [inverse, rhs]
    if extra is not None:
        in_specs.append(pl.BlockSpec((tile, half), lambda i, ids: (i, 0)))
        operands.append(extra)
    return pl.pallas_call(
        functools.partial(leaf_body, extra is not None),
        out_shape=struct(rows, half),
        grid_spec=pltpu.PrefetchScalarGridSpec(
            num_scalar_prefetch=1,
            grid=(steps,),
            in_specs=in_specs,
            out_specs=pl.BlockSpec((tile, half), lambda i, ids: (i, 0)),
            scratch_shapes=[pltpu.VMEM((depth, half), BF16)] * 2,
        ),
        compiler_params=pltpu.CompilerParams(vmem_limit_bytes=24 << 20),
        cost_estimate=pl.CostEstimate(
            flops=6 * rows * depth * half, bytes_accessed=4 * rows * half, transcendentals=0
        ),
    )(ids, *operands)


def pieces_body(arity, ids, own, got, *outs):
    member = ids[0] % arity
    width = outs[0].shape[1]
    for bits in range(arity):
        columns = pl.ds(pl.multiple_of((member ^ bits) * width, width), width)
        outs[bits][...] = own[:, columns] + got[:, columns]


def first_body(arity, ids, mine, near, near_other, far, far_other, joined, reduced):
    member, core = ids[0] % arity, ids[1]
    couple = reduced.shape[1]
    half = far.shape[0]
    joined[member] = mine[...]
    joined[member ^ (1 + core)] = near[...]
    joined[member ^ (2 - core)] = near_other[...]
    joined[member ^ 3, pl.ds(core * half, half)] = far[...]
    joined[member ^ 3, pl.ds((1 - core) * half, half)] = far_other[...]
    everything = joined[...].reshape(-1, joined.shape[-1])
    reduced[...] = dot_split(everything[:, couple:].T, everything[:, :couple])


def node_up_body(arity, ids, slots, reduced, *refs):
    pieces, (coeff, stack) = refs[:arity], refs[arity:]
    member, node = ids[0] % arity, ids[0] // arity
    rank = pieces[0].shape[0]
    for bits in range(arity):
        place = slots[node * arity + (member ^ bits)]
        stack[pl.ds(pl.multiple_of(place * rank, rank), rank)] = pieces[bits][...]
    coeff[...] = dot_split(reduced[...], stack[...])


def node_solve_body(arity, ids, slots, joined, stack, solve, basis):
    member, node = ids[0] % arity, ids[0] // arity
    couple = stack.shape[0]
    rank = joined.shape[1]
    high, low = split(stack[...])
    blocks = []
    for bits in range(arity):
        place = slots[node * arity + (member ^ bits)]
        block = joined[place]
        basis[bits * rank : (bits + 1) * rank] = block[:, couple:]
        blocks.append(block[:, :couple])
    left_high, left_low = split(jnp.concatenate(blocks, 0))
    solve[...] = dot(left_high, high) + dot(left_high, low) + dot(left_low, high)


def second_body(arity, share, root_rows, wide, ids, node_slots, *refs):
    inputs, outs, everything, root_all = refs[: 2 * arity], refs[2 * arity : -2], refs[-2], refs[-1]
    member, core = ids[0] % arity, ids[1]
    node = ids[0] // arity
    place = node % arity
    couple = outs[0].shape[1] if len(outs) == 1 else outs[1].shape[1]
    rank = everything.shape[1] - couple
    piece = min(wide, couple)
    height = inputs[0].shape[0] // 2
    for side in range(2):
        holder = core if side == 0 else 1 - core
        for bits in range(arity):
            ref = inputs[side * arity + bits]
            for half in range(2):
                distance = 2 * half + 1 - holder
                index = (place ^ distance) * arity + (member ^ bits)
                start = half * height
                everything[pl.ds(pl.multiple_of(index * share, share), share)] = ref[
                    start : start + share
                ]
                for part in range(wide // piece):
                    low = start + share + part * root_rows
                    root_all[
                        pl.ds(pl.multiple_of(index * root_rows, root_rows), root_rows),
                        part * piece : (part + 1) * piece,
                    ] = ref[low : low + root_rows, :piece]
    matrices = everything[...]
    reduced = dot_split(matrices[:, couple:].T, matrices[:, :couple])
    rows = everything[pl.ds(pl.multiple_of(node_slots[node] * rank, rank), rank)]
    if len(outs) == 1:
        root_coeff = dot_split(root_all[...], reduced)
        outs[0][...] = rows[:, :couple] - dot_split(rows[:, couple:], root_coeff)
    else:
        outs[0][...] = rows
        outs[1][...] = reduced
        outs[2][...] = root_all[...]


def place_second(arity, ids, node_slots, uppers, stack):
    node = ids[0] // arity
    rank = uppers[0].shape[0]
    for bits in range(arity):
        place = node_slots[node ^ bits]
        stack[pl.ds(pl.multiple_of(place * rank, rank), rank)] = uppers[bits][...]


def down_body(arity, ids, node_slots, down_map, solve, basis, *refs):
    uppers, outs, stack = refs[:arity], refs[arity:-1], refs[-1]
    place_second(arity, ids, node_slots, uppers, stack)
    upper_down = dot_split(down_map[...], stack[...])
    down = solve[...] - dot_split(basis[...], upper_down)
    rank = outs[0].shape[0]
    for bits in range(arity):
        outs[bits][...] = down[bits * rank : (bits + 1) * rank]


def stack_second_body(arity, ids, node_slots, *refs):
    place_second(arity, ids, node_slots, refs[:arity], refs[arity])


def subtract_body(arity, ids, upper_down, solve, basis, *outs):
    down = solve[...] - dot_split(basis[...], upper_down[...])
    rank = outs[0].shape[0]
    for bits in range(arity):
        outs[bits][...] = down[bits * rank : (bits + 1) * rank]


def final_body(arity, ids, base, basis, *refs):
    pieces, (out, high, low) = refs[:arity], refs[arity:]
    member = ids[0] % arity
    width = pieces[0].shape[1]

    @pl.when(pl.program_id(0) == 0)
    def _():
        for bits in range(arity):
            columns = pl.ds(pl.multiple_of((member ^ bits) * width, width), width)
            piece_high, piece_low = split(pieces[bits][...])
            high[:, columns] = piece_high
            low[:, columns] = piece_low

    left_high, left_low = split(basis[...])
    value = dot(left_high, high[...]) + dot(left_high, low[...]) + dot(left_low, high[...])
    out[...] = base[...] - value


def swap(block, bits):
    count = lax.axis_size("leaf")
    return lax.ppermute(block, "leaf", [(low, low ^ bits) for low in range(count)])


def swap_core(block):
    return lax.ppermute(block, "rhs", [(0, 1), (1, 0)])


def swap_each(block, bits):
    count = lax.axis_size("leaf")
    route = [
        (2 * low + core, 2 * (low ^ bits[core]) + core)
        for low in range(count)
        for core in range(2)
        if bits[core] is not None
    ]
    return lax.ppermute(block, ("leaf", "rhs"), route)


def per_device(
    rhs_block,
    leaf_inverse,
    leaf_basis,
    couple_one,
    basis_one,
    couple_two,
    basis_two,
    root_inverse,
    leaf_slot,
    node_slot,
):
    position = lax.axis_index("leaf")
    devices = lax.axis_size("leaf")
    core = lax.axis_index("rhs")
    points, rank = leaf_basis.shape
    couple = couple_one.shape[1]
    arity = couple // rank
    group = arity * arity
    tops = devices // group
    depth = rhs_block.shape[0]
    half = rhs_block.shape[1] // lax.axis_size("rhs")
    width = half // arity
    share = couple_two.shape[0]
    root_rows, wide = root_inverse.shape
    joined_width = couple + rank
    packed_rows = share + root_rows * (wide // min(wide, couple))
    ids = jnp.stack([position, core]).astype(jnp.int32)

    coeff_send, projected, joined_mine, packed = pl.pallas_call(
        coeff_send_body,
        out_shape=[
            struct(rank, half),
            struct(rank, depth),
            struct(rank, joined_width),
            struct(packed_rows, joined_width),
        ],
        grid_spec=pltpu.PrefetchScalarGridSpec(
            num_scalar_prefetch=1,
            grid=(arity,),
            in_specs=[
                whole(leaf_basis.shape),
                whole(leaf_inverse.shape),
                pl.BlockSpec((depth, width), lambda i, ids: (0, (1 - ids[1]) * arity + i)),
                whole(couple_one.shape),
                whole(basis_one.shape),
                whole(couple_two.shape),
                whole(basis_two.shape),
                whole(root_inverse.shape),
            ],
            out_specs=[
                pl.BlockSpec((rank, width), lambda i, ids: (0, i)),
                whole((rank, depth)),
                whole((rank, joined_width)),
                whole((packed_rows, joined_width)),
            ],
            scratch_shapes=[pltpu.VMEM((2 * rank, depth), BF16)],
        ),
        compiler_params=pltpu.CompilerParams(vmem_limit_bytes=20 << 20),
        cost_estimate=pl.CostEstimate(
            flops=6 * rank * depth * (points + half), bytes_accessed=6 << 20, transcendentals=0
        ),
    )(ids, leaf_basis, leaf_inverse, rhs_block, couple_one, basis_one, couple_two, basis_two, root_inverse)
    coeff_got = swap_core(coeff_send)
    coeff_own = pl.pallas_call(
        coeff_own_body,
        out_shape=struct(rank, half),
        grid_spec=pltpu.PrefetchScalarGridSpec(
            num_scalar_prefetch=1,
            grid=(arity,),
            in_specs=[
                whole((rank, depth)),
                pl.BlockSpec((depth, width), lambda i, ids: (0, ids[1] * arity + i)),
            ],
            out_specs=pl.BlockSpec((rank, width), lambda i, ids: (0, i)),
            scratch_shapes=[pltpu.VMEM((2 * rank, depth), BF16)],
        ),
        compiler_params=pltpu.CompilerParams(vmem_limit_bytes=16 << 20),
        cost_estimate=pl.CostEstimate(
            flops=6 * rank * depth * half, bytes_accessed=3 << 20, transcendentals=0
        ),
    )(ids, projected, rhs_block)

    near = swap_each(joined_mine, (1, 2))
    far = swap(lax.dynamic_slice_in_dim(joined_mine, core * (rank // 2), rank // 2, 0), 3)
    near_other = swap_core(near)
    far_other = swap_core(far)
    joined, reduced_one = call(
        functools.partial(first_body, arity),
        [struct(arity, rank, joined_width), struct(rank, couple)],
        [ids],
        [joined_mine, near, near_other, far, far_other],
        6 * couple * rank * couple,
    )

    pieces = call(
        functools.partial(pieces_body, arity),
        [struct(rank, width)] * arity,
        [ids],
        [coeff_own, coeff_got],
        rank * half,
    )
    pieces = [pieces[0]] + [swap(pieces[bits], bits) for bits in range(1, arity)]
    node_coeff, stack_one = call(
        functools.partial(node_up_body, arity),
        [struct(rank, width), struct(couple, width)],
        [ids, leaf_slot],
        [reduced_one, *pieces],
        6 * rank * couple * width,
    )
    uppers = [node_coeff] + [swap(node_coeff, arity * bits) for bits in range(1, arity)]
    node_solve, basis_rows = call(
        functools.partial(node_solve_body, arity),
        [struct(couple, width), struct(couple, rank)],
        [ids, leaf_slot],
        [joined, stack_one],
        6 * couple * couple * width,
    )

    two_near = swap_each(packed, (arity, 2 * arity))
    two_far = swap_each(packed, (3 * arity, None))
    two_mine = jnp.where(
        core == 0, jnp.concatenate([two_near, two_far], 0), jnp.concatenate([packed, two_near], 0)
    )
    two_got = [two_mine] + [swap(two_mine, bits) for bits in range(1, arity)]
    two_other = [swap_core(block) for block in two_got]
    if tops == 1:
        outs = [struct(rank, couple)]
    else:
        outs = [struct(rank, joined_width), struct(rank, couple), struct(rank, wide)]
    second = call(
        functools.partial(second_body, arity, share, root_rows, wide),
        outs,
        [ids, node_slot],
        [*two_got, *two_other],
        6 * couple * rank * couple,
        scratch=[pltpu.VMEM((couple, joined_width), F32), pltpu.VMEM((rank, wide), F32)],
    )
    if tops == 1:
        back = call(
            functools.partial(down_body, arity),
            [struct(rank, width)] * arity,
            [ids, node_slot],
            [second[0], node_solve, basis_rows, *uppers],
            12 * rank * couple * width,
            scratch=[pltpu.VMEM((couple, width), F32)],
        )
    else:
        mul = functools.partial(jnp.dot, precision=lax.Precision.HIGHEST)
        rows, reduced_two, root_all = second
        stack_two = call(
            functools.partial(stack_second_body, arity),
            [struct(couple, width)],
            [ids, node_slot],
            uppers,
            couple * width,
        )[0]
        upper_coeff = mul(reduced_two, stack_two)
        tops_coeff = jnp.stack(
            [upper_coeff] + [swap(upper_coeff, group * bits) for bits in range(1, tops)]
        )
        order = jnp.arange(tops, dtype=jnp.int32) ^ (position // group)
        tops_coeff = jnp.take(tops_coeff, order, axis=0).reshape(tops * rank, width)
        root_solve = mul(root_all, tops_coeff)
        upper_down = mul(rows[:, :couple], stack_two) - mul(rows[:, couple:], root_solve)
        back = call(
            functools.partial(subtract_body, arity),
            [struct(rank, width)] * arity,
            [ids],
            [upper_down, node_solve, basis_rows],
            6 * rank * couple * width,
        )
    back = [back[0]] + [swap(back[bits], bits) for bits in range(1, arity)]

    solve_got = swap_core(leaf_product(ids, leaf_inverse, rhs_block, half, False))
    base = leaf_product(ids, leaf_inverse, rhs_block, half, True, solve_got)
    tile = points // arity
    return pl.pallas_call(
        functools.partial(final_body, arity),
        out_shape=struct(points, half),
        grid_spec=pltpu.PrefetchScalarGridSpec(
            num_scalar_prefetch=1,
            grid=(arity,),
            in_specs=[
                pl.BlockSpec((tile, half), lambda i, ids: (i, 0)),
                pl.BlockSpec((tile, rank), lambda i, ids: (i, 0)),
            ]
            + [whole((rank, width))] * arity,
            out_specs=pl.BlockSpec((tile, half), lambda i, ids: (i, 0)),
            scratch_shapes=[pltpu.VMEM((rank, half), BF16)] * 2,
        ),
        compiler_params=pltpu.CompilerParams(vmem_limit_bytes=16 << 20),
        cost_estimate=pl.CostEstimate(
            flops=6 * points * rank * half, bytes_accessed=8 * points * half, transcendentals=0
        ),
    )(ids, base, leaf_basis, *back)


def solution(mesh):
    return jax.shard_map(
        per_device,
        mesh=mesh,
        in_specs=(
            P(("leaf", "rhs"), None),
            P("leaf", "rhs"),
            P("leaf", None),
            P("leaf", None),
            P("leaf", None),
            P("leaf", None),
            P("leaf", None),
            P("leaf", None),
            P(),
            P(),
        ),
        out_specs=P("leaf", "rhs"),
        check_vma=False,
    )
```

```python
import functools

import jax
import jax.numpy as jnp
from jax import lax
from jax.experimental import pallas as pl
from jax.experimental.pallas import tpu as pltpu
from jax.sharding import PartitionSpec as P


F32 = jnp.float32
BF16 = jnp.bfloat16


def split(value):
    high = value.astype(BF16)
    return high, (value - high.astype(F32)).astype(BF16)


def dot(left, right):
    return jnp.dot(left, right, preferred_element_type=F32)


def dot_parts(left_high, left_low, right_high, right_low):
    rows = left_high.shape[0]
    both = dot(jnp.concatenate([left_high, left_low], 0), right_high)
    return both[:rows] + both[rows:] + dot(left_high, right_low)


def dot_split(left, right):
    return dot_parts(*split(left), *split(right))


def call(body, out_shapes, scalars, operands, flops, limit_mib=16, scratch=()):
    moved = sum(o.size * o.dtype.itemsize for o in list(operands) + list(out_shapes))
    vmem = pl.BlockSpec(memory_space=pltpu.VMEM)
    return pl.pallas_call(
        body,
        out_shape=out_shapes,
        in_specs=[pl.BlockSpec(memory_space=pltpu.SMEM)] * len(scalars) + [vmem] * len(operands),
        out_specs=[vmem] * len(out_shapes),
        scratch_shapes=scratch,
        compiler_params=pltpu.CompilerParams(vmem_limit_bytes=limit_mib << 20),
        cost_estimate=pl.CostEstimate(flops=flops, bytes_accessed=moved, transcendentals=0),
    )(*scalars, *operands)


def struct(*shape, dtype=F32):
    return jax.ShapeDtypeStruct(shape, dtype)


def coeff_body(
    arity, ids, basis, inverse, rhs, couple_one, basis_one, couple_two, basis_two, root,
    send, own, inverse_high, inverse_low, other_high, other_low, own_high, own_low, joined, packed, mixed,
    basis_here, inverse_here, rhs_here, turned, projected, sems,
):
    member, core = ids[0] % arity, ids[1]
    rank, half = send.shape
    width = half // arity
    couple = couple_one.shape[1]
    share = couple_two.shape[0]
    root_rows, wide = root.shape
    piece = min(wide, couple)
    chunk = basis.shape[0] // arity
    count = iter(range(sems.shape[0]))

    def fetch(source, target):
        copy = pltpu.make_async_copy(source, target, sems.at[next(count)])
        copy.start()
        return copy

    basis_copy = fetch(basis, basis_here)
    inverse_copies = [
        fetch(inverse.at[step * chunk : (step + 1) * chunk], inverse_here.at[step * chunk : (step + 1) * chunk])
        for step in range(arity)
    ]
    rhs_copies = []
    for side in range(2):
        for bits in range(arity):
            column = (((1 - core) if side == 0 else core) * arity + (member ^ bits)) * width
            at = (side * arity + bits) * width
            rhs_copies.append(
                fetch(rhs.at[:, pl.ds(pl.multiple_of(column, width), width)], rhs_here.at[:, at : at + width])
            )
            if side == 0 and bits == arity - 1:
                matrix_copies = [
                    fetch(couple_one, joined.at[:, :couple]),
                    fetch(basis_one, joined.at[:, couple:]),
                    fetch(couple_two, packed.at[:share, :couple]),
                    fetch(basis_two, packed.at[:share, couple:]),
                ]
                for part in range(wide // piece):
                    low = share + part * root_rows
                    matrix_copies.append(
                        fetch(
                            root.at[:, part * piece : (part + 1) * piece],
                            packed.at[low : low + root_rows, :piece],
                        )
                    )

    packed[share:, piece:] = jnp.zeros_like(packed[share:, piece:])
    basis_copy.wait()
    high, low = split(basis_here[...].T)
    turned[:rank] = high
    turned[rank:] = low
    both = first = 0.0
    for step in range(arity):
        rows = slice(step * chunk, (step + 1) * chunk)
        inverse_copies[step].wait()
        high, low = split(inverse_here[rows])
        inverse_high[rows] = high
        inverse_low[rows] = low
        both = both + dot(turned[:, rows], high)
        first = first + dot(turned[:rank, rows], low)
    high, low = split(both[:rank] + both[rank:] + first)
    projected[:rank] = high
    projected[rank:] = low
    for side, (out, out_high, out_low) in enumerate(((send, other_high, other_low), (own, own_high, own_low))):
        for bits in range(arity):
            at = (side * arity + bits) * width
            columns = slice(bits * width, (bits + 1) * width)
            rhs_copies[side * arity + bits].wait()
            high, low = split(rhs_here[:, at : at + width])
            out_high[:, columns] = high
            out_low[:, columns] = low
            both = dot(projected[...], high)
            out[:, columns] = both[:rank] + both[rank:] + dot(projected[:rank], low)
    for copy in matrix_copies:
        copy.wait()

    @pl.when(core == 0)
    def _():
        mixed[...] = joined[...]

    @pl.when(core != 0)
    def _():
        mixed[: packed.shape[0]] = packed[...]
        mixed[packed.shape[0] :] = jnp.zeros_like(mixed[packed.shape[0] :])


def leaf_body(add, inverse_high, inverse_low, rhs_high, rhs_low, *rest):
    out = rest[-1]
    tile = out.shape[0] // 4

    @pl.loop(0, 4)
    def _(step):
        rows = pl.ds(pl.multiple_of(step * tile, tile), tile)
        left_high, left_low = inverse_high[rows], inverse_low[rows]
        value = dot(left_high, rhs_high[...]) + dot(left_high, rhs_low[...]) + dot(left_low, rhs_high[...])
        out[rows] = value + rest[0][rows] if add else value


def leaf_product(inverse, rhs, extra=()):
    rows, depth = inverse[0].shape
    half = rhs[0].shape[1]
    return call(
        functools.partial(leaf_body, len(extra) > 0),
        [struct(rows, half)],
        [],
        [*inverse, *rhs, *extra],
        6 * rows * depth * half,
    )[0]


def pieces_body(own, got, *outs):
    width = outs[0].shape[1]
    for bits, out in enumerate(outs):
        columns = slice(bits * width, (bits + 1) * width)
        out[...] = own[:, columns] + got[:, columns]


def first_body(arity, ids, mine, near, near_other, mixed, mixed_other, joined, reduced):
    member, core = ids[0] % arity, ids[1]
    couple = reduced.shape[1]
    joined[member] = mine[...]
    joined[member ^ (1 + core)] = near[...]
    joined[member ^ (2 - core)] = near_other[...]

    @pl.when(core == 0)
    def _():
        joined[member ^ 3] = mixed[...]

    @pl.when(core != 0)
    def _():
        joined[member ^ 3] = mixed_other[...]

    everything = joined[...].reshape(-1, joined.shape[-1])
    reduced[...] = dot_split(everything[:, couple:].T, everything[:, :couple])


def column_body(arity, share, root_rows, wide, ids, packed, mixed, mixed_other, rest, rest_other, column, part):
    node, core = ids[0] // arity, ids[1]
    place = node % arity
    rank = column.shape[1] - wide_couple(share, arity)
    couple = column.shape[1] - rank
    piece = min(wide, couple)
    units = wide // piece
    lanes = couple // piece

    def put(distance, ref):
        index = place ^ distance
        column[pl.ds(pl.multiple_of(index * share, share), share)] = ref[:share]
        for unit in range(units):
            number = index * units + unit
            strip, lane = number // lanes, number % lanes
            column[
                pl.ds(pl.multiple_of(arity * share + strip * root_rows, root_rows), root_rows),
                pl.ds(pl.multiple_of(lane * piece, piece), piece),
            ] = ref[share + unit * root_rows : share + (unit + 1) * root_rows, :piece]

    column[arity * share :] = jnp.zeros_like(column[arity * share :])
    put(0, packed)

    @pl.when(core == 0)
    def _():
        put(1, mixed_other)
        put(2, rest)
        put(3, rest_other)

    @pl.when(core != 0)
    def _():
        put(1, mixed)
        put(2, rest_other)
        put(3, rest)

    height = part.shape[0]
    part[...] = column[pl.ds(pl.multiple_of(core * height, 8), height)]


def wide_couple(share, arity):
    return share * arity * arity


def node_up_body(arity, ids, slots, reduced, *refs):
    pieces, (coeff, stack) = refs[:arity], refs[arity:]
    member, node = ids[0] % arity, ids[0] // arity
    rank = pieces[0].shape[0]
    for bits in range(arity):
        place = slots[node * arity + (member ^ bits)]
        stack[pl.ds(pl.multiple_of(place * rank, rank), rank)] = pieces[bits][...]
    coeff[...] = dot_split(reduced[...], stack[...])


def node_solve_body(arity, ids, slots, joined, stack, solve, basis):
    member, node = ids[0] % arity, ids[0] // arity
    couple = stack.shape[0]
    rank = joined.shape[1]
    high, low = split(stack[...])
    blocks = []
    for bits in range(arity):
        place = slots[node * arity + (member ^ bits)]
        block = joined[place]
        basis[bits * rank : (bits + 1) * rank] = block[:, couple:]
        blocks.append(block[:, :couple])
    left_high, left_low = split(jnp.concatenate(blocks, 0))
    solve[...] = dot(left_high, high) + dot(left_high, low) + dot(left_low, high)


def second_body(arity, share, root_rows, wide, ids, node_slots, mine, near, near_other, far, far_other, *refs):
    outs, everything, root_all = refs[:-2], refs[-2], refs[-1]
    member, core = ids[0] % arity, ids[1]
    node = ids[0] // arity
    couple = wide_couple(share, arity)
    rank = everything.shape[1] - couple
    piece = min(wide, couple)
    units = wide // piece
    lanes = couple // piece

    def put(distance, pieces):
        def rows(start, count):
            ref = pieces[start // pieces[0].shape[0]]
            start = start % pieces[0].shape[0]
            return ref[start : start + count]

        for place in range(arity):
            index = place * arity + (member ^ distance)
            for low in range(0, share, 8):
                everything[pl.ds(pl.multiple_of(index * share + low, 8), 8)] = rows(place * share + low, 8)
            for unit in range(units):
                number = place * units + unit
                strip, lane = number // lanes, number % lanes
                root_all[
                    pl.ds(pl.multiple_of(index * root_rows, root_rows), root_rows),
                    unit * piece : (unit + 1) * piece,
                ] = rows(arity * share + strip * root_rows, root_rows)[:, lane * piece : (lane + 1) * piece]

    put(0, [mine])

    @pl.when(core == 0)
    def _():
        put(1, [near])
        put(2, [near_other])
        put(3, [far, far_other])

    @pl.when(core != 0)
    def _():
        put(1, [near_other])
        put(2, [near])
        put(3, [far_other, far])

    matrices = everything[...]
    reduced = dot_split(matrices[:, couple:].T, matrices[:, :couple])
    rows = everything[pl.ds(pl.multiple_of(node_slots[node] * rank, rank), rank)]
    if len(outs) == 1:
        root_coeff = dot_split(root_all[...], reduced)
        outs[0][...] = rows[:, :couple] - dot_split(rows[:, couple:], root_coeff)
    else:
        outs[0][...] = rows
        outs[1][...] = reduced
        outs[2][...] = root_all[...]


def place_second(arity, ids, node_slots, uppers, stack):
    node = ids[0] // arity
    rank = uppers[0].shape[0]
    for bits in range(arity):
        place = node_slots[node ^ bits]
        stack[pl.ds(pl.multiple_of(place * rank, rank), rank)] = uppers[bits][...]


def down_body(arity, ids, node_slots, down_map, solve, basis, *refs):
    uppers, outs, stack = refs[:arity], refs[arity:-1], refs[-1]
    place_second(arity, ids, node_slots, uppers, stack)
    upper_down = dot_split(down_map[...], stack[...])
    down = solve[...] - dot_split(basis[...], upper_down)
    rank = outs[0].shape[0]
    for bits in range(arity):
        outs[bits][...] = down[bits * rank : (bits + 1) * rank]


def stack_second_body(arity, ids, node_slots, *refs):
    place_second(arity, ids, node_slots, refs[:arity], refs[arity])


def subtract_body(arity, ids, upper_down, solve, basis, *outs):
    down = solve[...] - dot_split(basis[...], upper_down[...])
    rank = outs[0].shape[0]
    for bits in range(arity):
        outs[bits][...] = down[bits * rank : (bits + 1) * rank]


def final_body(arity, ids, base, basis, *refs):
    pieces, (out, left, high, low) = refs[:arity], refs[arity:]
    step = pl.program_id(0)
    rank = pieces[0].shape[0]

    @pl.when(step == 0)
    def _():
        left_high, left_low = split(basis[...])
        left[:, :rank] = left_high
        left[:, rank:] = left_low
        for bits in range(arity):
            piece_high, piece_low = split(pieces[bits][...])
            high[bits, :rank] = piece_high
            high[bits, rank:] = piece_high
            low[bits] = piece_low

    width = out.shape[1]
    columns = pl.ds(pl.multiple_of(step * width, width), width)
    out[...] = base[:, columns] - (dot(left[...], high[step]) + dot(left[:, :rank], low[step]))


def swap(block, bits):
    count = lax.axis_size("leaf")
    return lax.ppermute(block, "leaf", [(low, low ^ bits) for low in range(count)])


def swap_core(block):
    return lax.ppermute(block, "rhs", [(0, 1), (1, 0)])


def swap_each(block, bits):
    count = lax.axis_size("leaf")
    route = [
        (2 * low + core, 2 * (low ^ bits[core]) + core)
        for low in range(count)
        for core in range(2)
        if bits[core] is not None
    ]
    return lax.ppermute(block, ("leaf", "rhs"), route)


def per_device(
    rhs_block,
    leaf_inverse,
    leaf_basis,
    couple_one,
    basis_one,
    couple_two,
    basis_two,
    root_inverse,
    leaf_slot,
    node_slot,
):
    position = lax.axis_index("leaf")
    devices = lax.axis_size("leaf")
    core = lax.axis_index("rhs")
    points, rank = leaf_basis.shape
    couple = couple_one.shape[1]
    arity = couple // rank
    group = arity * arity
    tops = devices // group
    depth = rhs_block.shape[0]
    half = rhs_block.shape[1] // lax.axis_size("rhs")
    width = half // arity
    share = couple_two.shape[0]
    root_rows, wide = root_inverse.shape
    joined_width = couple + rank
    packed_rows = share + root_rows * (wide // min(wide, couple))
    ids = jnp.stack([position, core]).astype(jnp.int32)

    vmem = pl.BlockSpec(memory_space=pltpu.VMEM)
    large = [leaf_basis, leaf_inverse, rhs_block, couple_one, basis_one, couple_two, basis_two, root_inverse]
    coeff = pl.pallas_call(
        functools.partial(coeff_body, arity),
        out_shape=[struct(rank, half)] * 2
        + [struct(points, depth, dtype=BF16)] * 2
        + [struct(depth, half, dtype=BF16)] * 4
        + [struct(rank, joined_width), struct(packed_rows, joined_width), struct(rank, joined_width)],
        in_specs=[pl.BlockSpec(memory_space=pltpu.SMEM)] + [pl.BlockSpec(memory_space=pl.ANY)] * len(large),
        out_specs=[vmem] * 11,
        scratch_shapes=[
            pltpu.VMEM((points, rank), F32),
            pltpu.VMEM((points, depth), F32),
            pltpu.VMEM((depth, 2 * half), F32),
            pltpu.VMEM((2 * rank, points), BF16),
            pltpu.VMEM((2 * rank, depth), BF16),
            pltpu.SemaphoreType.DMA((5 + 3 * arity + wide // min(wide, couple),)),
        ],
        compiler_params=pltpu.CompilerParams(vmem_limit_bytes=16 << 20),
        cost_estimate=pl.CostEstimate(
            flops=6 * rank * depth * (points + 2 * half), bytes_accessed=14 << 20, transcendentals=0
        ),
    )
    coeff_send, coeff_own, *halves, joined_mine, packed, mixed_mine = coeff(
        ids, *[pltpu.with_memory_space_constraint(array, pltpu.HBM) for array in large]
    )
    inverse_parts, rhs_other, rhs_own = halves[:2], halves[2:4], halves[4:]
    coeff_got = swap_core(coeff_send)

    near = swap_each(joined_mine, (1, 2))
    mixed = swap_each(mixed_mine, (3, arity))
    rest = swap_each(packed, (2 * arity, 3 * arity))

    near_other = swap_core(near)
    mixed_other = swap_core(mixed)
    rest_other = swap_core(rest)
    joined, reduced_one = call(
        functools.partial(first_body, arity),
        [struct(arity, rank, joined_width), struct(rank, couple)],
        [ids],
        [joined_mine, near, near_other, mixed, mixed_other],
        6 * couple * rank * couple,
    )

    column_rows = arity * share + root_rows * (arity * wide // couple)
    column_half = -(-column_rows // 16) * 8
    column, column_part = call(
        functools.partial(column_body, arity, share, root_rows, wide),
        [struct(2 * column_half, joined_width), struct(column_half, joined_width)],
        [ids],
        [packed, mixed, mixed_other, rest, rest_other],
        0,
    )
    column_near = swap_each(column, (1, 2))
    column_far = swap(column_part, 3)
    column_near_other = swap_core(column_near)
    column_far_other = swap_core(column_far)

    pieces = call(pieces_body, [struct(rank, width)] * arity, [], [coeff_own, coeff_got], rank * half)
    pieces = [pieces[0]] + [swap(pieces[bits], bits) for bits in range(1, arity)]
    node_coeff, stack_one = call(
        functools.partial(node_up_body, arity),
        [struct(rank, width), struct(couple, width)],
        [ids, leaf_slot],
        [reduced_one, *pieces],
        6 * rank * couple * width,
    )
    uppers = [node_coeff] + [swap(node_coeff, arity * bits) for bits in range(1, arity)]
    node_solve, basis_rows = call(
        functools.partial(node_solve_body, arity),
        [struct(couple, width), struct(couple, rank)],
        [ids, leaf_slot],
        [joined, stack_one],
        6 * couple * couple * width,
    )

    if tops == 1:
        outs = [struct(rank, couple)]
    else:
        outs = [struct(rank, joined_width), struct(rank, couple), struct(rank, wide)]
    second = call(
        functools.partial(second_body, arity, share, root_rows, wide),
        outs,
        [ids, node_slot],
        [column, column_near, column_near_other, column_far, column_far_other],
        6 * couple * rank * couple,
        scratch=[pltpu.VMEM((couple, joined_width), F32), pltpu.VMEM((rank, wide), F32)],
    )
    if tops == 1:
        back = call(
            functools.partial(down_body, arity),
            [struct(rank, width)] * arity,
            [ids, node_slot],
            [second[0], node_solve, basis_rows, *uppers],
            12 * rank * couple * width,
            scratch=[pltpu.VMEM((couple, width), F32)],
        )
    else:
        mul = functools.partial(jnp.dot, precision=lax.Precision.HIGHEST)
        rows, reduced_two, root_all = second
        stack_two = call(
            functools.partial(stack_second_body, arity),
            [struct(couple, width)],
            [ids, node_slot],
            uppers,
            couple * width,
        )[0]
        upper_coeff = mul(reduced_two, stack_two)
        tops_coeff = jnp.stack([upper_coeff] + [swap(upper_coeff, group * bits) for bits in range(1, tops)])
        order = jnp.arange(tops, dtype=jnp.int32) ^ (position // group)
        tops_coeff = jnp.take(tops_coeff, order, axis=0).reshape(tops * rank, width)
        root_solve = mul(root_all, tops_coeff)
        upper_down = mul(rows[:, :couple], stack_two) - mul(rows[:, couple:], root_solve)
        back = call(
            functools.partial(subtract_body, arity),
            [struct(rank, width)] * arity,
            [ids],
            [upper_down, node_solve, basis_rows],
            6 * rank * couple * width,
        )
    back = [back[0]] + [swap(back[bits], bits) for bits in range(1, arity)]

    solve_got = swap_core(leaf_product(inverse_parts, rhs_other))
    base = leaf_product(inverse_parts, rhs_own, [solve_got])
    return pl.pallas_call(
        functools.partial(final_body, arity),
        out_shape=struct(points, half),
        grid_spec=pltpu.PrefetchScalarGridSpec(
            num_scalar_prefetch=1,
            grid=(arity,),
            in_specs=[vmem] * (2 + arity),
            out_specs=pl.BlockSpec((points, width), lambda i, ids: (0, (ids[0] % arity) ^ i)),
            scratch_shapes=[
                pltpu.VMEM((points, 2 * rank), BF16),
                pltpu.VMEM((arity, 2 * rank, width), BF16),
                pltpu.VMEM((arity, rank, width), BF16),
            ],
        ),
        compiler_params=pltpu.CompilerParams(vmem_limit_bytes=16 << 20),
        cost_estimate=pl.CostEstimate(
            flops=6 * points * rank * half, bytes_accessed=8 * points * half, transcendentals=0
        ),
    )(ids, base, leaf_basis, *back)


def solution(mesh):
    return jax.shard_map(
        per_device,
        mesh=mesh,
        in_specs=(
            P(("leaf", "rhs"), None),
            P("leaf", "rhs"),
            P("leaf", None),
            P("leaf", None),
            P("leaf", None),
            P("leaf", None),
            P("leaf", None),
            P("leaf", None),
            P(),
            P(),
        ),
        out_specs=P("leaf", "rhs"),
        check_vma=False,
    )
```

```python
import functools

import jax
import jax.numpy as jnp
from jax import lax
from jax.experimental import pallas as pl
from jax.experimental.pallas import tpu as pltpu
from jax.sharding import PartitionSpec as P


F32 = jnp.float32
BF16 = jnp.bfloat16


def split(value):
    high = value.astype(BF16)
    return high, (value - high.astype(F32)).astype(BF16)


def dot(left, right):
    return jnp.dot(left, right, preferred_element_type=F32)


def dot_parts(left_high, left_low, right_high, right_low):
    rows = left_high.shape[0]
    both = dot(jnp.concatenate([left_high, left_low], 0), right_high)
    return both[:rows] + both[rows:] + dot(left_high, right_low)


def dot_split(left, right):
    return dot_parts(*split(left), *split(right))


def call(body, out_shapes, scalars, operands, flops, limit_mib=16, scratch=()):
    moved = sum(o.size * o.dtype.itemsize for o in list(operands) + list(out_shapes))
    vmem = pl.BlockSpec(memory_space=pltpu.VMEM)
    return pl.pallas_call(
        body,
        out_shape=out_shapes,
        in_specs=[pl.BlockSpec(memory_space=pltpu.SMEM)] * len(scalars) + [vmem] * len(operands),
        out_specs=[vmem] * len(out_shapes),
        scratch_shapes=scratch,
        compiler_params=pltpu.CompilerParams(vmem_limit_bytes=limit_mib << 20),
        cost_estimate=pl.CostEstimate(flops=flops, bytes_accessed=moved, transcendentals=0),
    )(*scalars, *operands)


def struct(*shape, dtype=F32):
    return jax.ShapeDtypeStruct(shape, dtype)


def coeff_body(
    arity, ids, basis, inverse, rhs, couple_one, basis_one, couple_two, basis_two, root,
    send, own, basis_parts, inverse_high, inverse_low, other_high, other_low, own_high, own_low, joined, packed, mixed,
    basis_here, inverse_here, rhs_here, turned, projected, sems,
):
    member, core = ids[0] % arity, ids[1]
    rank, half = send.shape
    width = half // arity
    couple = couple_one.shape[1]
    share = couple_two.shape[0]
    root_rows, wide = root.shape
    piece = min(wide, couple)
    chunk = basis.shape[0] // arity
    count = iter(range(sems.shape[0]))

    def fetch(source, target):
        copy = pltpu.make_async_copy(source, target, sems.at[next(count)])
        copy.start()
        return copy

    basis_copy = fetch(basis, basis_here)
    inverse_copies = [
        fetch(inverse.at[step * chunk : (step + 1) * chunk], inverse_here.at[step * chunk : (step + 1) * chunk])
        for step in range(arity)
    ]
    rhs_copies = []
    for side in range(2):
        for bits in range(arity):
            column = (((1 - core) if side == 0 else core) * arity + (member ^ bits)) * width
            at = (side * arity + bits) * width
            rhs_copies.append(
                fetch(rhs.at[:, pl.ds(pl.multiple_of(column, width), width)], rhs_here.at[:, at : at + width])
            )
            if side == 0 and bits == arity - 1:
                matrix_copies = [
                    fetch(couple_one, joined.at[:, :couple]),
                    fetch(basis_one, joined.at[:, couple:]),
                    fetch(couple_two, packed.at[:share, :couple]),
                    fetch(basis_two, packed.at[:share, couple:]),
                ]
                for part in range(wide // piece):
                    low = share + part * root_rows
                    matrix_copies.append(
                        fetch(
                            root.at[:, part * piece : (part + 1) * piece],
                            packed.at[low : low + root_rows, :piece],
                        )
                    )

    packed[share:, piece:] = jnp.zeros_like(packed[share:, piece:])

    def parts(source, rows, columns, out_high, out_low, out_columns):
        for low_row in range(rows.start, rows.stop, 64):
            at = slice(low_row, low_row + 64)
            high, low = split(source[at, columns])
            out_high[at, out_columns] = high
            out_low[at, out_columns] = low

    basis_copy.wait()
    points = basis.shape[0]
    for low_row in range(0, points, rank):
        at = slice(low_row, low_row + rank)
        value = basis_here[at]
        high, low = split(value)
        basis_parts[at, :rank] = high
        basis_parts[at, rank : 2 * rank] = low
        basis_parts[at, 2 * rank :] = high
        high, low = split(value.T)
        turned[:rank, at] = high
        turned[rank:, at] = low
    for step in range(arity):
        inverse_copies[step].wait()
        everything = slice(0, inverse.shape[1])
        parts(
            inverse_here, slice(step * chunk, (step + 1) * chunk), everything, inverse_high, inverse_low, everything
        )
    depth = inverse.shape[1]
    blocks = [
        (side, bits, out, out_high, out_low)
        for side, (out, out_high, out_low) in enumerate(((send, other_high, other_low), (own, own_high, own_low)))
        for bits in range(arity)
    ]

    def prepare(number):
        side, bits, _, out_high, out_low = blocks[number]
        at = (side * arity + bits) * width
        columns = slice(bits * width, (bits + 1) * width)
        parts(rhs_here, slice(0, depth), slice(at, at + width), out_high, out_low, columns)

    def multiply(number):
        _, bits, out, out_high, out_low = blocks[number]
        columns = slice(bits * width, (bits + 1) * width)
        both = dot(projected[...], out_high[:, columns])
        out[:, columns] = both[:rank] + both[rank:] + dot(projected[:rank], out_low[:, columns])

    for number in range(2):
        rhs_copies[number].wait()
    for low_column in range(0, depth, width):
        columns = slice(low_column, low_column + width)
        both = dot(turned[...], inverse_high[:, columns])
        high, low = split(both[:rank] + both[rank:] + dot(turned[:rank], inverse_low[:, columns]))
        projected[:rank, columns] = high
        projected[rank:, columns] = low
    prepare(0)
    prepare(1)
    for number in range(0, len(blocks), 2):
        later = range(number + 2, min(number + 4, len(blocks)))
        for other in later:
            rhs_copies[other].wait()
        multiply(number)
        multiply(number + 1)
        for other in later:
            prepare(other)
    for copy in matrix_copies:
        copy.wait()

    @pl.when(core == 0)
    def _():
        mixed[...] = joined[...]

    @pl.when(core != 0)
    def _():
        mixed[: packed.shape[0]] = packed[...]
        mixed[packed.shape[0] :] = jnp.zeros_like(mixed[packed.shape[0] :])


def leaf_body(add, inverse_high, inverse_low, rhs_high, rhs_low, *rest):
    out = rest[-1]
    tile = out.shape[0] // 4

    @pl.loop(0, 4)
    def _(step):
        rows = pl.ds(pl.multiple_of(step * tile, tile), tile)
        left_high, left_low = inverse_high[rows], inverse_low[rows]
        value = dot(left_high, rhs_high[...]) + dot(left_high, rhs_low[...]) + dot(left_low, rhs_high[...])
        out[rows] = value + rest[0][rows] if add else value


def leaf_product(inverse, rhs, extra=()):
    rows, depth = inverse[0].shape
    half = rhs[0].shape[1]
    return call(
        functools.partial(leaf_body, len(extra) > 0),
        [struct(rows, half)],
        [],
        [*inverse, *rhs, *extra],
        6 * rows * depth * half,
    )[0]


def pieces_body(own, got, *outs):
    width = outs[0].shape[1]
    for bits, out in enumerate(outs):
        columns = slice(bits * width, (bits + 1) * width)
        out[...] = own[:, columns] + got[:, columns]


def first_body(arity, ids, mine, one, one_other, two, two_other, joined, reduced):
    member, core = ids[0] % arity, ids[1]
    couple = reduced.shape[1] // 3
    joined[member] = mine[...]

    @pl.when(core == 0)
    def _():
        joined[member ^ 1] = one[...]
        joined[member ^ 2] = two[...]
        joined[member ^ 3] = two_other[...]

    @pl.when(core != 0)
    def _():
        joined[member ^ 1] = one_other[...]
        joined[member ^ 2] = two_other[...]
        joined[member ^ 3] = two[...]

    everything = joined[...].reshape(-1, joined.shape[-1])
    high, low = split(dot_split(everything[:, couple:].T, everything[:, :couple]))
    reduced[:, :couple] = high
    reduced[:, couple : 2 * couple] = low
    reduced[:, 2 * couple :] = high


def column_body(arity, share, root_rows, wide, ids, packed, one, one_other, three, three_other, column, part):
    node, core = ids[0] // arity, ids[1]
    place = node % arity
    rank = column.shape[1] - wide_couple(share, arity)
    couple = column.shape[1] - rank
    piece = min(wide, couple)
    units = wide // piece
    lanes = couple // piece

    def put(distance, ref):
        index = place ^ distance
        column[pl.ds(pl.multiple_of(index * share, share), share)] = ref[:share]
        for unit in range(units):
            number = index * units + unit
            strip, lane = number // lanes, number % lanes
            column[
                pl.ds(pl.multiple_of(arity * share + strip * root_rows, root_rows), root_rows),
                pl.ds(pl.multiple_of(lane * piece, piece), piece),
            ] = ref[share + unit * root_rows : share + (unit + 1) * root_rows, :piece]

    column[arity * share :] = jnp.zeros_like(column[arity * share :])
    put(0, packed)

    @pl.when(core == 0)
    def _():
        put(1, one_other)
        put(2, three)
        put(3, three_other)

    @pl.when(core != 0)
    def _():
        put(1, one)
        put(2, three_other)
        put(3, three)

    height = part.shape[0]
    part[...] = column[pl.ds(pl.multiple_of(core * height, 8), height)]


def wide_couple(share, arity):
    return share * arity * arity


def node_up_body(arity, ids, slots, reduced, *refs):
    pieces, (coeff, stack) = refs[:arity], refs[arity:]
    member, node = ids[0] % arity, ids[0] // arity
    rank = pieces[0].shape[0]
    couple = arity * rank
    for bits in range(arity):
        place = slots[node * arity + (member ^ bits)]
        high, low = split(pieces[bits][...])
        for part, value in enumerate((high, high, low)):
            stack[pl.ds(pl.multiple_of(part * couple + place * rank, rank), rank)] = value
    coeff[...] = dot(reduced[...], stack[...])


def node_solve_body(arity, ids, slots, joined, stack, solve, basis):
    member, node = ids[0] % arity, ids[0] // arity
    couple = stack.shape[0] // 3
    rank = joined.shape[1]
    blocks = []
    for bits in range(arity):
        place = slots[node * arity + (member ^ bits)]
        block = joined[place]
        basis[bits * rank : (bits + 1) * rank] = block[:, couple:]
        blocks.append(block[:, :couple])
    left_high, left_low = split(jnp.concatenate(blocks, 0))
    solve[...] = dot(jnp.concatenate([left_high, left_low, left_high], 1), stack[...])


def second_body(arity, share, root_rows, wide, ids, node_slots, mine, near, near_other, far, far_other, basis_rows, *refs):
    outs, everything, root_all = refs[:-2], refs[-2], refs[-1]
    member, core = ids[0] % arity, ids[1]
    node = ids[0] // arity
    couple = wide_couple(share, arity)
    rank = everything.shape[1] - couple
    piece = min(wide, couple)
    units = wide // piece
    lanes = couple // piece

    def put(distance, pieces):
        def rows(start, count):
            ref = pieces[start // pieces[0].shape[0]]
            start = start % pieces[0].shape[0]
            return ref[start : start + count]

        for place in range(arity):
            index = place * arity + (member ^ distance)
            for low in range(0, share, 8):
                everything[pl.ds(pl.multiple_of(index * share + low, 8), 8)] = rows(place * share + low, 8)
            for unit in range(units):
                number = place * units + unit
                strip, lane = number // lanes, number % lanes
                root_all[
                    pl.ds(pl.multiple_of(index * root_rows, root_rows), root_rows),
                    unit * piece : (unit + 1) * piece,
                ] = rows(arity * share + strip * root_rows, root_rows)[:, lane * piece : (lane + 1) * piece]

    put(0, [mine])

    @pl.when(core == 0)
    def _():
        put(1, [near])
        put(2, [near_other])
        put(3, [far, far_other])

    @pl.when(core != 0)
    def _():
        put(1, [near_other])
        put(2, [near])
        put(3, [far_other, far])

    matrices = everything[...]
    reduced = dot_split(matrices[:, couple:].T, matrices[:, :couple])
    rows = everything[pl.ds(pl.multiple_of(node_slots[node] * rank, rank), rank)]
    if len(outs) == 1:
        root_coeff = dot_split(root_all[...], reduced)
        down_map = rows[:, :couple] - dot_split(rows[:, couple:], root_coeff)
        left_high, left_low = split(basis_rows[...])
        high, low = split(down_map)
        high, low = split(dot(left_high, high) + dot(left_high, low) + dot(left_low, high))
        outs[0][:, :couple] = high
        outs[0][:, couple : 2 * couple] = low
        outs[0][:, 2 * couple :] = high
    else:
        outs[0][...] = rows
        outs[1][...] = reduced
        outs[2][...] = root_all[...]


def second_rows(arity, ids, node_slots, bits, rank):
    place = node_slots[ids[0] // arity ^ bits]
    return pl.ds(pl.multiple_of(place * rank, rank), rank)


def down_body(arity, ids, node_slots, down_map, solve, *refs):
    uppers, outs, stack = refs[:arity], refs[arity:-1], refs[-1]
    rank = outs[0].shape[0]
    couple = arity * rank
    for bits in range(arity):
        place = node_slots[ids[0] // arity ^ bits]
        high, low = split(uppers[bits][...])
        for part, value in enumerate((high, high, low)):
            stack[pl.ds(pl.multiple_of(part * couple + place * rank, rank), rank)] = value
    for bits in range(arity):
        rows = slice(bits * rank, (bits + 1) * rank)
        outs[bits][...] = solve[rows] - dot(down_map[rows], stack[...])


def stack_second_body(arity, ids, node_slots, *refs):
    for bits in range(arity):
        refs[arity][second_rows(arity, ids, node_slots, bits, refs[0].shape[0])] = refs[bits][...]


def subtract_body(arity, ids, upper_down, solve, basis, *outs):
    down = solve[...] - dot_split(basis[...], upper_down[...])
    rank = outs[0].shape[0]
    for bits in range(arity):
        outs[bits][...] = down[bits * rank : (bits + 1) * rank]


def final_body(first, arity, ids, base, left, *refs):
    here, right, sems = refs[-3:]
    out = refs[-4]
    pieces = [ref for ref in refs[:-4] if 3 * ref.shape[0] == left.shape[1]]
    member = ids[0] % arity
    rank, width = pieces[0].shape
    parts = sems.shape[1]
    tall = here.shape[0] // parts
    copies = []
    for number, piece in enumerate(pieces):
        columns = slice(number * width, (number + 1) * width)
        source = slice((number + first) * width, (number + first + 1) * width)
        high, low = split(piece[...])
        right[:rank, columns] = high
        right[rank : 2 * rank, columns] = high
        right[2 * rank :, columns] = low
        target = pl.ds(pl.multiple_of((member ^ (number + first)) * width, width), width)
        for part in range(parts):
            rows = slice(part * tall, (part + 1) * tall)
            here[rows, columns] = base[rows, source] - dot(left[rows], right[:, columns])
            copy = pltpu.make_async_copy(here.at[rows, columns], out.at[rows, target], sems.at[number, part])
            copy.start()
            copies.append(copy)
    for copy in copies:
        copy.wait()


def final(ids, base, left, first, pieces, so_far=None):
    rank, width = pieces[0].shape
    points, half = base.shape
    vmem = pl.BlockSpec(memory_space=pltpu.VMEM)
    hbm = pl.BlockSpec(memory_space=pltpu.HBM)
    more = [] if so_far is None else [so_far]
    return pl.pallas_call(
        functools.partial(final_body, first, half // width),
        out_shape=struct(points, half),
        in_specs=[pl.BlockSpec(memory_space=pltpu.SMEM)] + [vmem] * (2 + len(pieces)) + [hbm] * len(more),
        out_specs=hbm,
        scratch_shapes=[
            pltpu.VMEM((points, len(pieces) * width), F32),
            pltpu.VMEM((3 * rank, len(pieces) * width), BF16),
            pltpu.SemaphoreType.DMA((len(pieces), 4)),
        ],
        input_output_aliases={3 + len(pieces): 0} if more else {},
        compiler_params=pltpu.CompilerParams(vmem_limit_bytes=16 << 20),
        cost_estimate=pl.CostEstimate(
            flops=6 * points * rank * width * len(pieces),
            bytes_accessed=8 * points * width * len(pieces),
            transcendentals=0,
        ),
    )(ids, base, left, *pieces, *more)


def swap(block, bits):
    count = lax.axis_size("leaf")
    return lax.ppermute(block, "leaf", [(low, low ^ bits) for low in range(count)])


def swap_core(block):
    return lax.ppermute(block, "rhs", [(0, 1), (1, 0)])


def swap_each(block, bits):
    count = lax.axis_size("leaf")
    route = [
        (2 * low + core, 2 * (low ^ bits[core]) + core)
        for low in range(count)
        for core in range(2)
        if bits[core] is not None
    ]
    return lax.ppermute(block, ("leaf", "rhs"), route)


def per_device(
    rhs_block,
    leaf_inverse,
    leaf_basis,
    couple_one,
    basis_one,
    couple_two,
    basis_two,
    root_inverse,
    leaf_slot,
    node_slot,
):
    position = lax.axis_index("leaf")
    devices = lax.axis_size("leaf")
    core = lax.axis_index("rhs")
    points, rank = leaf_basis.shape
    couple = couple_one.shape[1]
    arity = couple // rank
    group = arity * arity
    tops = devices // group
    depth = rhs_block.shape[0]
    half = rhs_block.shape[1] // lax.axis_size("rhs")
    width = half // arity
    share = couple_two.shape[0]
    root_rows, wide = root_inverse.shape
    joined_width = couple + rank
    packed_rows = share + root_rows * (wide // min(wide, couple))
    ids = jnp.stack([position, core]).astype(jnp.int32)

    vmem = pl.BlockSpec(memory_space=pltpu.VMEM)
    large = [leaf_basis, leaf_inverse, rhs_block, couple_one, basis_one, couple_two, basis_two, root_inverse]
    coeff = pl.pallas_call(
        functools.partial(coeff_body, arity),
        out_shape=[struct(rank, half)] * 2
        + [struct(points, 3 * rank, dtype=BF16)]
        + [struct(points, depth, dtype=BF16)] * 2
        + [struct(depth, half, dtype=BF16)] * 4
        + [struct(rank, joined_width), struct(packed_rows, joined_width), struct(rank, joined_width)],
        in_specs=[pl.BlockSpec(memory_space=pltpu.SMEM)] + [pl.BlockSpec(memory_space=pl.ANY)] * len(large),
        out_specs=[vmem] * 12,
        scratch_shapes=[
            pltpu.VMEM((points, rank), F32),
            pltpu.VMEM((points, depth), F32),
            pltpu.VMEM((depth, 2 * half), F32),
            pltpu.VMEM((2 * rank, points), BF16),
            pltpu.VMEM((2 * rank, depth), BF16),
            pltpu.SemaphoreType.DMA((5 + 3 * arity + wide // min(wide, couple),)),
        ],
        compiler_params=pltpu.CompilerParams(vmem_limit_bytes=16 << 20),
        cost_estimate=pl.CostEstimate(
            flops=6 * rank * depth * (points + 2 * half), bytes_accessed=14 << 20, transcendentals=0
        ),
    )
    coeff_send, coeff_own, basis_parts, *halves, joined_mine, packed, mixed_mine = coeff(
        ids, *[pltpu.with_memory_space_constraint(array, pltpu.HBM) for array in large]
    )
    inverse_parts, rhs_other, rhs_own = halves[:2], halves[2:4], halves[4:]
    coeff_got = swap_core(coeff_send)

    one = swap_each(mixed_mine, (1, arity))
    two = swap_each(joined_mine, (2, 3))
    three = swap_each(packed, (2 * arity, 3 * arity))
    one_other = swap_core(one)
    two_other = swap_core(two)
    three_other = swap_core(three)
    joined, reduced_one = call(
        functools.partial(first_body, arity),
        [struct(arity, rank, joined_width), struct(rank, 3 * couple, dtype=BF16)],
        [ids],
        [joined_mine, one, one_other, two, two_other],
        6 * couple * rank * couple,
    )
    column_rows = arity * share + root_rows * (arity * wide // couple)
    column_half = -(-column_rows // 16) * 8
    column, column_part = call(
        functools.partial(column_body, arity, share, root_rows, wide),
        [struct(2 * column_half, joined_width), struct(column_half, joined_width)],
        [ids],
        [packed, one, one_other, three, three_other],
        0,
    )
    column_near = swap_each(column, (1, 2))
    column_far = swap(column_part, 3)
    column_near_other = swap_core(column_near)
    column_far_other = swap_core(column_far)

    pieces = call(pieces_body, [struct(rank, width)] * arity, [], [coeff_own, coeff_got], rank * half)
    pieces = [pieces[0]] + [swap(pieces[bits], bits) for bits in range(1, arity)]
    node_coeff, stack_one = call(
        functools.partial(node_up_body, arity),
        [struct(rank, width), struct(3 * couple, width, dtype=BF16)],
        [ids, leaf_slot],
        [reduced_one, *pieces],
        6 * rank * couple * width,
    )
    uppers = [node_coeff] + [swap(node_coeff, arity * bits) for bits in range(1, arity)]
    node_solve, basis_rows = call(
        functools.partial(node_solve_body, arity),
        [struct(couple, width), struct(couple, rank)],
        [ids, leaf_slot],
        [joined, stack_one],
        6 * couple * couple * width,
    )

    if tops == 1:
        outs = [struct(couple, 3 * couple, dtype=BF16)]
    else:
        outs = [struct(rank, joined_width), struct(rank, couple), struct(rank, wide)]
    second = call(
        functools.partial(second_body, arity, share, root_rows, wide),
        outs,
        [ids, node_slot],
        [column, column_near, column_near_other, column_far, column_far_other, basis_rows],
        6 * couple * rank * couple,
        scratch=[pltpu.VMEM((couple, joined_width), F32), pltpu.VMEM((rank, wide), F32)],
    )
    if tops == 1:
        back = call(
            functools.partial(down_body, arity),
            [struct(rank, width)] * arity,
            [ids, node_slot],
            [*second, node_solve, *uppers],
            6 * couple * couple * width,
            scratch=[pltpu.VMEM((3 * couple, width), BF16)],
        )
    else:
        mul = functools.partial(jnp.dot, precision=lax.Precision.HIGHEST)
        rows, reduced_two, root_all = second
        stack_two = call(
            functools.partial(stack_second_body, arity),
            [struct(couple, width)],
            [ids, node_slot],
            uppers,
            couple * width,
        )[0]
        upper_coeff = mul(reduced_two, stack_two)
        tops_coeff = jnp.stack([upper_coeff] + [swap(upper_coeff, group * bits) for bits in range(1, tops)])
        order = jnp.arange(tops, dtype=jnp.int32) ^ (position // group)
        tops_coeff = jnp.take(tops_coeff, order, axis=0).reshape(tops * rank, width)
        root_solve = mul(root_all, tops_coeff)
        upper_down = mul(rows[:, :couple], stack_two) - mul(rows[:, couple:], root_solve)
        back = call(
            functools.partial(subtract_body, arity),
            [struct(rank, width)] * arity,
            [ids],
            [upper_down, node_solve, basis_rows],
            6 * rank * couple * width,
        )
    back = [back[0]] + [swap(back[bits], bits) for bits in range(1, arity)]

    solve_got = swap_core(leaf_product(inverse_parts, rhs_other))
    base = leaf_product(inverse_parts, rhs_own, [solve_got])
    so_far = final(ids, base, basis_parts, 0, back[:1])
    return final(ids, base, basis_parts, 1, back[1:], so_far)


def solution(mesh):
    return jax.shard_map(
        per_device,
        mesh=mesh,
        in_specs=(
            P(("leaf", "rhs"), None),
            P("leaf", "rhs"),
            P("leaf", None),
            P("leaf", None),
            P("leaf", None),
            P("leaf", None),
            P("leaf", None),
            P("leaf", None),
            P(),
            P(),
        ),
        out_specs=P("leaf", "rhs"),
        check_vma=False,
    )
```

```python
import functools

import jax
import jax.numpy as jnp
from jax import lax
from jax.experimental import pallas as pl
from jax.experimental.pallas import tpu as pltpu
from jax.sharding import PartitionSpec as P


F32 = jnp.float32
BF16 = jnp.bfloat16


def split(value):
    high = value.astype(BF16)
    return high, (value - high.astype(F32)).astype(BF16)


def dot(left, right):
    return jnp.dot(left, right, preferred_element_type=F32)


def dot_parts(left_high, left_low, right_high, right_low):
    rows = left_high.shape[0]
    both = dot(jnp.concatenate([left_high, left_low], 0), right_high)
    return both[:rows] + both[rows:] + dot(left_high, right_low)


def dot_split(left, right):
    return dot_parts(*split(left), *split(right))


def call(body, out_shapes, scalars, operands, flops, limit_mib=16, scratch=()):
    moved = sum(o.size * o.dtype.itemsize for o in list(operands) + list(out_shapes))
    vmem = pl.BlockSpec(memory_space=pltpu.VMEM)
    return pl.pallas_call(
        body,
        out_shape=out_shapes,
        in_specs=[pl.BlockSpec(memory_space=pltpu.SMEM)] * len(scalars) + [vmem] * len(operands),
        out_specs=[vmem] * len(out_shapes),
        scratch_shapes=scratch,
        compiler_params=pltpu.CompilerParams(vmem_limit_bytes=limit_mib << 20),
        cost_estimate=pl.CostEstimate(flops=flops, bytes_accessed=moved, transcendentals=0),
    )(*scalars, *operands)


def struct(*shape, dtype=F32):
    return jax.ShapeDtypeStruct(shape, dtype)


def pack_body(ids, couple_one, basis_one, couple_two, basis_two, root, joined, packed, mixed, sems):
    couple = couple_one.shape[1]
    share = couple_two.shape[0]
    root_rows, wide = root.shape
    piece = min(wide, couple)
    moves = [
        (couple_one, joined.at[:, :couple]),
        (basis_one, joined.at[:, couple:]),
        (couple_two, packed.at[:share, :couple]),
        (basis_two, packed.at[:share, couple:]),
    ]
    for part in range(wide // piece):
        low = share + part * root_rows
        moves.append(
            (root.at[:, part * piece : (part + 1) * piece], packed.at[low : low + root_rows, :piece])
        )
    copies = [pltpu.make_async_copy(*move, sems.at[number]) for number, move in enumerate(moves)]
    for copy in copies:
        copy.start()
    packed[share:, piece:] = jnp.zeros_like(packed[share:, piece:])
    for copy in copies:
        copy.wait()

    @pl.when(ids[1] == 0)
    def _():
        mixed[...] = joined[...]

    @pl.when(ids[1] != 0)
    def _():
        mixed[: packed.shape[0]] = packed[...]
        mixed[packed.shape[0] :] = jnp.zeros_like(mixed[packed.shape[0] :])


def coeff_body(
    arity, ids, basis, inverse, rhs,
    send, own, basis_parts, inverse_high, inverse_low, other_high, other_low, own_high, own_low,
    turned, projected,
):
    member, core = ids[0] % arity, ids[1]
    rank, half = send.shape
    width = half // arity
    chunk = basis.shape[0] // arity

    def parts(source, rows, columns, out_high, out_low, out_columns):
        for low_row in range(rows.start, rows.stop, 64):
            at = slice(low_row, low_row + 64)
            high, low = split(source[at, columns])
            out_high[at, out_columns] = high
            out_low[at, out_columns] = low

    points = basis.shape[0]
    for low_row in range(0, points, rank):
        at = slice(low_row, low_row + rank)
        value = basis[at]
        high, low = split(value)
        basis_parts[at, :rank] = high
        basis_parts[at, rank : 2 * rank] = low
        basis_parts[at, 2 * rank :] = high
        high, low = split(value.T)
        turned[:rank, at] = high
        turned[rank:, at] = low
    for step in range(arity):
        everything = slice(0, inverse.shape[1])
        parts(
            inverse, slice(step * chunk, (step + 1) * chunk), everything, inverse_high, inverse_low, everything
        )
    depth = inverse.shape[1]
    blocks = [
        (side, bits, out, out_high, out_low)
        for side, (out, out_high, out_low) in enumerate(((send, other_high, other_low), (own, own_high, own_low)))
        for bits in range(arity)
    ]

    def prepare(number):
        side, bits, _, out_high, out_low = blocks[number]
        place = (((1 - core) if side == 0 else core) * arity + (member ^ bits)) * width
        columns = slice(bits * width, (bits + 1) * width)
        parts(rhs, slice(0, depth), pl.ds(pl.multiple_of(place, width), width), out_high, out_low, columns)

    def multiply(number):
        _, bits, out, out_high, out_low = blocks[number]
        columns = slice(bits * width, (bits + 1) * width)
        both = dot(projected[...], out_high[:, columns])
        out[:, columns] = both[:rank] + both[rank:] + dot(projected[:rank], out_low[:, columns])

    for low_column in range(0, depth, width):
        columns = slice(low_column, low_column + width)
        both = dot(turned[...], inverse_high[:, columns])
        high, low = split(both[:rank] + both[rank:] + dot(turned[:rank], inverse_low[:, columns]))
        projected[:rank, columns] = high
        projected[rank:, columns] = low
    prepare(0)
    prepare(1)
    for number in range(0, len(blocks), 2):
        later = range(number + 2, min(number + 4, len(blocks)))
        multiply(number)
        multiply(number + 1)
        for other in later:
            prepare(other)


def leaf_body(add, inverse_high, inverse_low, rhs_high, rhs_low, *rest):
    out = rest[-1]
    tiles = 2
    tile = out.shape[0] // tiles

    @pl.loop(0, tiles)
    def _(step):
        rows = pl.ds(pl.multiple_of(step * tile, tile), tile)
        left_high, left_low = inverse_high[rows], inverse_low[rows]
        value = dot(left_high, rhs_high[...]) + dot(left_high, rhs_low[...]) + dot(left_low, rhs_high[...])
        out[rows] = value + rest[0][rows] if add else value


def leaf_product(inverse, rhs, extra=()):
    rows, depth = inverse[0].shape
    half = rhs[0].shape[1]
    return call(
        functools.partial(leaf_body, len(extra) > 0),
        [struct(rows, half)],
        [],
        [*inverse, *rhs, *extra],
        6 * rows * depth * half,
    )[0]


def pieces_body(own, got, *outs):
    width = outs[0].shape[1]
    for bits, out in enumerate(outs):
        columns = slice(bits * width, (bits + 1) * width)
        out[...] = own[:, columns] + got[:, columns]


def first_body(arity, ids, mine, one, one_other, two, two_other, joined, reduced):
    member, core = ids[0] % arity, ids[1]
    couple = reduced.shape[1] // 3
    joined[member] = mine[...]

    @pl.when(core == 0)
    def _():
        joined[member ^ 1] = one[...]
        joined[member ^ 2] = two[...]
        joined[member ^ 3] = two_other[...]

    @pl.when(core != 0)
    def _():
        joined[member ^ 1] = one_other[...]
        joined[member ^ 2] = two_other[...]
        joined[member ^ 3] = two[...]

    everything = joined[...].reshape(-1, joined.shape[-1])
    high, low = split(dot_split(everything[:, couple:].T, everything[:, :couple]))
    reduced[:, :couple] = high
    reduced[:, couple : 2 * couple] = low
    reduced[:, 2 * couple :] = high


def column_body(arity, share, root_rows, wide, ids, packed, one, one_other, three, three_other, column, part):
    node, core = ids[0] // arity, ids[1]
    place = node % arity
    rank = column.shape[1] - wide_couple(share, arity)
    couple = column.shape[1] - rank
    piece = min(wide, couple)
    units = wide // piece
    lanes = couple // piece

    def put(distance, ref):
        index = place ^ distance
        column[pl.ds(pl.multiple_of(index * share, share), share)] = ref[:share]
        for unit in range(units):
            number = index * units + unit
            strip, lane = number // lanes, number % lanes
            column[
                pl.ds(pl.multiple_of(arity * share + strip * root_rows, root_rows), root_rows),
                pl.ds(pl.multiple_of(lane * piece, piece), piece),
            ] = ref[share + unit * root_rows : share + (unit + 1) * root_rows, :piece]

    column[arity * share :] = jnp.zeros_like(column[arity * share :])
    put(0, packed)

    @pl.when(core == 0)
    def _():
        put(1, one_other)
        put(2, three)
        put(3, three_other)

    @pl.when(core != 0)
    def _():
        put(1, one)
        put(2, three_other)
        put(3, three)

    height = part.shape[0]
    part[...] = column[pl.ds(pl.multiple_of(core * height, 8), height)]


def wide_couple(share, arity):
    return share * arity * arity


def node_up_body(arity, ids, slots, reduced, *refs):
    pieces, (coeff, stack) = refs[:arity], refs[arity:]
    member, node = ids[0] % arity, ids[0] // arity
    rank = pieces[0].shape[0]
    couple = arity * rank
    for bits in range(arity):
        place = slots[node * arity + (member ^ bits)]
        high, low = split(pieces[bits][...])
        for part, value in enumerate((high, high, low)):
            stack[pl.ds(pl.multiple_of(part * couple + place * rank, rank), rank)] = value
    coeff[...] = dot(reduced[...], stack[...])


def node_solve_body(arity, ids, slots, joined, stack, solve, basis):
    member, node = ids[0] % arity, ids[0] // arity
    couple = stack.shape[0] // 3
    rank = joined.shape[1]
    blocks = []
    for bits in range(arity):
        place = slots[node * arity + (member ^ bits)]
        block = joined[place]
        basis[bits * rank : (bits + 1) * rank] = block[:, couple:]
        blocks.append(block[:, :couple])
    left_high, left_low = split(jnp.concatenate(blocks, 0))
    solve[...] = dot(jnp.concatenate([left_high, left_low, left_high], 1), stack[...])


def second_body(arity, share, root_rows, wide, ids, node_slots, mine, near, near_other, far, far_other, basis_rows, *refs):
    outs, everything, root_all = refs[:-2], refs[-2], refs[-1]
    member, core = ids[0] % arity, ids[1]
    node = ids[0] // arity
    couple = wide_couple(share, arity)
    rank = everything.shape[1] - couple
    piece = min(wide, couple)
    units = wide // piece
    lanes = couple // piece

    def put(distance, pieces):
        def rows(start, count):
            ref = pieces[start // pieces[0].shape[0]]
            start = start % pieces[0].shape[0]
            return ref[start : start + count]

        for place in range(arity):
            index = place * arity + (member ^ distance)
            for low in range(0, share, 8):
                everything[pl.ds(pl.multiple_of(index * share + low, 8), 8)] = rows(place * share + low, 8)
            for unit in range(units):
                number = place * units + unit
                strip, lane = number // lanes, number % lanes
                root_all[
                    pl.ds(pl.multiple_of(index * root_rows, root_rows), root_rows),
                    unit * piece : (unit + 1) * piece,
                ] = rows(arity * share + strip * root_rows, root_rows)[:, lane * piece : (lane + 1) * piece]

    put(0, [mine])

    @pl.when(core == 0)
    def _():
        put(1, [near])
        put(2, [near_other])
        put(3, [far, far_other])

    @pl.when(core != 0)
    def _():
        put(1, [near_other])
        put(2, [near])
        put(3, [far_other, far])

    matrices = everything[...]
    reduced = dot_split(matrices[:, couple:].T, matrices[:, :couple])
    rows = everything[pl.ds(pl.multiple_of(node_slots[node] * rank, rank), rank)]
    if len(outs) == 1:
        root_coeff = dot_split(root_all[...], reduced)
        down_map = rows[:, :couple] - dot_split(rows[:, couple:], root_coeff)
        left_high, left_low = split(basis_rows[...])
        high, low = split(down_map)
        high, low = split(dot(left_high, high) + dot(left_high, low) + dot(left_low, high))
        outs[0][:, :couple] = high
        outs[0][:, couple : 2 * couple] = low
        outs[0][:, 2 * couple :] = high
    else:
        outs[0][...] = rows
        outs[1][...] = reduced
        outs[2][...] = root_all[...]


def second_rows(arity, ids, node_slots, bits, rank):
    place = node_slots[ids[0] // arity ^ bits]
    return pl.ds(pl.multiple_of(place * rank, rank), rank)


def down_body(arity, ids, node_slots, down_map, solve, *refs):
    uppers, outs, stack = refs[:arity], refs[arity:-1], refs[-1]
    rank = outs[0].shape[0]
    couple = arity * rank
    for bits in range(arity):
        place = node_slots[ids[0] // arity ^ bits]
        high, low = split(uppers[bits][...])
        for part, value in enumerate((high, high, low)):
            stack[pl.ds(pl.multiple_of(part * couple + place * rank, rank), rank)] = value
    for bits in range(0, arity, 2):
        rows = slice(bits * rank, (bits + 2) * rank)
        down = solve[rows] - dot(down_map[rows], stack[...])
        outs[bits][...] = down[:rank]
        outs[bits + 1][...] = down[rank:]


def stack_second_body(arity, ids, node_slots, *refs):
    for bits in range(arity):
        refs[arity][second_rows(arity, ids, node_slots, bits, refs[0].shape[0])] = refs[bits][...]


def subtract_body(arity, ids, upper_down, solve, basis, *outs):
    down = solve[...] - dot_split(basis[...], upper_down[...])
    rank = outs[0].shape[0]
    for bits in range(arity):
        outs[bits][...] = down[bits * rank : (bits + 1) * rank]


def final_body(first, arity, ids, base, left, *refs):
    here, right, sems = refs[-3:]
    out = refs[-4]
    pieces = [ref for ref in refs[:-4] if 3 * ref.shape[0] == left.shape[1]]
    member = ids[0] % arity
    rank, width = pieces[0].shape
    parts = sems.shape[1]
    tall = here.shape[0] // parts
    copies = []
    for number, piece in enumerate(pieces):
        columns = slice(number * width, (number + 1) * width)
        source = slice((number + first) * width, (number + first + 1) * width)
        high, low = split(piece[...])
        right[:rank, columns] = high
        right[rank : 2 * rank, columns] = high
        right[2 * rank :, columns] = low
        target = pl.ds(pl.multiple_of((member ^ (number + first)) * width, width), width)
        for part in range(parts):
            rows = slice(part * tall, (part + 1) * tall)
            here[rows, columns] = base[rows, source] - dot(left[rows], right[:, columns])
            copy = pltpu.make_async_copy(here.at[rows, columns], out.at[rows, target], sems.at[number, part])
            copy.start()
            copies.append(copy)
    for copy in copies:
        copy.wait()


def final(ids, base, left, first, pieces, so_far=None):
    rank, width = pieces[0].shape
    points, half = base.shape
    vmem = pl.BlockSpec(memory_space=pltpu.VMEM)
    hbm = pl.BlockSpec(memory_space=pltpu.HBM)
    more = [] if so_far is None else [so_far]
    return pl.pallas_call(
        functools.partial(final_body, first, half // width),
        out_shape=struct(points, half),
        in_specs=[pl.BlockSpec(memory_space=pltpu.SMEM)] + [vmem] * (2 + len(pieces)) + [hbm] * len(more),
        out_specs=hbm,
        scratch_shapes=[
            pltpu.VMEM((points, len(pieces) * width), F32),
            pltpu.VMEM((3 * rank, len(pieces) * width), BF16),
            pltpu.SemaphoreType.DMA((len(pieces), 4)),
        ],
        input_output_aliases={3 + len(pieces): 0} if more else {},
        compiler_params=pltpu.CompilerParams(vmem_limit_bytes=16 << 20),
        cost_estimate=pl.CostEstimate(
            flops=6 * points * rank * width * len(pieces),
            bytes_accessed=8 * points * width * len(pieces),
            transcendentals=0,
        ),
    )(ids, base, left, *pieces, *more)


def swap(block, bits):
    count = lax.axis_size("leaf")
    return lax.ppermute(block, "leaf", [(low, low ^ bits) for low in range(count)])


def swap_core(block):
    return lax.ppermute(block, "rhs", [(0, 1), (1, 0)])


def swap_each(block, bits):
    count = lax.axis_size("leaf")
    route = [
        (2 * low + core, 2 * (low ^ bits[core]) + core)
        for low in range(count)
        for core in range(2)
        if bits[core] is not None
    ]
    return lax.ppermute(block, ("leaf", "rhs"), route)


def per_device(
    rhs_block,
    leaf_inverse,
    leaf_basis,
    couple_one,
    basis_one,
    couple_two,
    basis_two,
    root_inverse,
    leaf_slot,
    node_slot,
):
    position = lax.axis_index("leaf")
    devices = lax.axis_size("leaf")
    core = lax.axis_index("rhs")
    points, rank = leaf_basis.shape
    couple = couple_one.shape[1]
    arity = couple // rank
    group = arity * arity
    tops = devices // group
    depth = rhs_block.shape[0]
    half = rhs_block.shape[1] // lax.axis_size("rhs")
    width = half // arity
    share = couple_two.shape[0]
    root_rows, wide = root_inverse.shape
    joined_width = couple + rank
    packed_rows = share + root_rows * (wide // min(wide, couple))
    ids = jnp.stack([position, core]).astype(jnp.int32)

    vmem = pl.BlockSpec(memory_space=pltpu.VMEM)
    hbm = pl.BlockSpec(memory_space=pl.ANY)

    def in_hbm(arrays):
        return [pltpu.with_memory_space_constraint(array, pltpu.HBM) for array in arrays]

    matrices = [couple_one, basis_one, couple_two, basis_two, root_inverse]
    pack = pl.pallas_call(
        pack_body,
        out_shape=[struct(rank, joined_width), struct(packed_rows, joined_width), struct(rank, joined_width)],
        in_specs=[pl.BlockSpec(memory_space=pltpu.SMEM)] + [hbm] * len(matrices),
        out_specs=[vmem] * 3,
        scratch_shapes=[pltpu.SemaphoreType.DMA((4 + wide // min(wide, couple),))],
        compiler_params=pltpu.CompilerParams(vmem_limit_bytes=16 << 20),
        cost_estimate=pl.CostEstimate(flops=20_000_000_000, bytes_accessed=20 << 20, transcendentals=0),
    )
    joined_mine, packed, mixed_mine = pack(ids, *in_hbm(matrices))
    one = swap_each(mixed_mine, (1, arity))
    two = swap_each(joined_mine, (2, 3))
    three = swap_each(packed, (2 * arity, 3 * arity))

    large = [leaf_basis, leaf_inverse, rhs_block]
    coeff = pl.pallas_call(
        functools.partial(coeff_body, arity),
        out_shape=[struct(rank, half)] * 2
        + [struct(points, 3 * rank, dtype=BF16)]
        + [struct(points, depth, dtype=BF16)] * 2
        + [struct(depth, half, dtype=BF16)] * 4,
        in_specs=[pl.BlockSpec(memory_space=pltpu.SMEM)] + [vmem] * len(large),
        out_specs=[vmem] * 9,
        scratch_shapes=[
            pltpu.VMEM((2 * rank, points), BF16),
            pltpu.VMEM((2 * rank, depth), BF16),
        ],
        compiler_params=pltpu.CompilerParams(vmem_limit_bytes=16 << 20),
        cost_estimate=pl.CostEstimate(
            flops=6 * rank * depth * (points + 2 * half), bytes_accessed=14 << 20, transcendentals=0
        ),
    )
    coeff_send, coeff_own, basis_parts, *halves = coeff(ids, *large)
    inverse_parts, rhs_other, rhs_own = halves[:2], halves[2:4], halves[4:]
    coeff_got = swap_core(coeff_send)

    one_other = swap_core(one)
    two_other = swap_core(two)
    three_other = swap_core(three)
    joined, reduced_one = call(
        functools.partial(first_body, arity),
        [struct(arity, rank, joined_width), struct(rank, 3 * couple, dtype=BF16)],
        [ids],
        [joined_mine, one, one_other, two, two_other],
        6 * couple * rank * couple,
    )
    column_rows = arity * share + root_rows * (arity * wide // couple)
    column_half = -(-column_rows // 16) * 8
    column, column_part = call(
        functools.partial(column_body, arity, share, root_rows, wide),
        [struct(2 * column_half, joined_width), struct(column_half, joined_width)],
        [ids],
        [packed, one, one_other, three, three_other],
        0,
    )
    column_near = swap_each(column, (1, 2))
    column_far = swap(column_part, 3)
    column_near_other = swap_core(column_near)
    column_far_other = swap_core(column_far)

    pieces = call(pieces_body, [struct(rank, width)] * arity, [], [coeff_own, coeff_got], rank * half)
    pieces = [pieces[0]] + [swap(pieces[bits], bits) for bits in range(1, arity)]
    node_coeff, stack_one = call(
        functools.partial(node_up_body, arity),
        [struct(rank, width), struct(3 * couple, width, dtype=BF16)],
        [ids, leaf_slot],
        [reduced_one, *pieces],
        6 * rank * couple * width,
    )
    uppers = [node_coeff] + [swap(node_coeff, arity * bits) for bits in range(1, arity)]
    node_solve, basis_rows = call(
        functools.partial(node_solve_body, arity),
        [struct(couple, width), struct(couple, rank)],
        [ids, leaf_slot],
        [joined, stack_one],
        6 * couple * couple * width,
    )

    if tops == 1:
        outs = [struct(couple, 3 * couple, dtype=BF16)]
    else:
        outs = [struct(rank, joined_width), struct(rank, couple), struct(rank, wide)]
    second = call(
        functools.partial(second_body, arity, share, root_rows, wide),
        outs,
        [ids, node_slot],
        [column, column_near, column_near_other, column_far, column_far_other, basis_rows],
        6 * couple * rank * couple,
        scratch=[pltpu.VMEM((couple, joined_width), F32), pltpu.VMEM((rank, wide), F32)],
    )
    if tops == 1:
        back = call(
            functools.partial(down_body, arity),
            [struct(rank, width)] * arity,
            [ids, node_slot],
            [*second, node_solve, *uppers],
            6 * couple * couple * width,
            scratch=[pltpu.VMEM((3 * couple, width), BF16)],
        )
    else:
        mul = functools.partial(jnp.dot, precision=lax.Precision.HIGHEST)
        rows, reduced_two, root_all = second
        stack_two = call(
            functools.partial(stack_second_body, arity),
            [struct(couple, width)],
            [ids, node_slot],
            uppers,
            couple * width,
        )[0]
        upper_coeff = mul(reduced_two, stack_two)
        tops_coeff = jnp.stack([upper_coeff] + [swap(upper_coeff, group * bits) for bits in range(1, tops)])
        order = jnp.arange(tops, dtype=jnp.int32) ^ (position // group)
        tops_coeff = jnp.take(tops_coeff, order, axis=0).reshape(tops * rank, width)
        root_solve = mul(root_all, tops_coeff)
        upper_down = mul(rows[:, :couple], stack_two) - mul(rows[:, couple:], root_solve)
        back = call(
            functools.partial(subtract_body, arity),
            [struct(rank, width)] * arity,
            [ids],
            [upper_down, node_solve, basis_rows],
            6 * rank * couple * width,
        )
    back = [back[0]] + [swap(back[bits], bits) for bits in range(1, arity)]

    solve_got = swap_core(leaf_product(inverse_parts, rhs_other))
    base = leaf_product(inverse_parts, rhs_own, [solve_got])
    so_far = final(ids, base, basis_parts, 0, back[:1])
    return final(ids, base, basis_parts, 1, back[1:], so_far)


def solution(mesh):
    return jax.shard_map(
        per_device,
        mesh=mesh,
        in_specs=(
            P(("leaf", "rhs"), None),
            P("leaf", "rhs"),
            P("leaf", None),
            P("leaf", None),
            P("leaf", None),
            P("leaf", None),
            P("leaf", None),
            P("leaf", None),
            P(),
            P(),
        ),
        out_specs=P("leaf", "rhs"),
        check_vma=False,
    )
```
